128 devices in a mesh: dp: 16 (over x, y), bag: 8 (over z, core).
Axes of the slice: x: 4, y: 4, z: 4, core: 2. Of those that a mesh axis runs over, the one named last changes fastest.
Arguments:
- home_tokens: bfloat16 [16384, 3072], P('dp', 'bag'), may hold values from -6 to 6
- mod_weight: bfloat16 [2, 3072, 3072], P(None, None, 'bag'), may hold values from -0.109375 to 0.109375
- qkv_weight: bfloat16 [3, 3072, 3072], P(None, None, 'bag')
- norm_gain: float32 [2, 3072], P(None, 'bag'), may hold values from 0.5 to 8
- output_weight: bfloat16 [3072, 3072], P('bag'), may hold values from -0.109375 to 0.109375
- row_plan: int32 [16384], replicated, may hold values from 0 to 20479, as said below
- sample_lengths: int32 [16, 4], replicated, may hold values from 0 to 1280, as said below
- modality: int32 [16, 4], replicated, may hold values from 0 to 1
Outputs:
- block_output: bfloat16 [16384, 3072], P('dp', 'bag')
The draws below stay inside these ranges and needn't reach their ends.
Inputs may be any that keep to these rules, and one draw needn't show every extreme that they name: `row_plan`: row r sits on home r // 1024; no two rows share a value; the rows of bag j fill exactly its slots 0 to sample_ends[j, 3] - 1; no home sends more than 128 rows to one bag, and some home sends exactly 128 rows to some bag. `sample_lengths`: row j lists the lengths of the samples of bag j in slot order, zeros allowed; each row sums to at most 1280, and some bag holds one sample of 1280 tokens.
All inputs are finite; a program needn't handle non-finite values.
Results may differ from the reference program's by a relative error of at most 0.013.
The reference program's roundings to bfloat16 on the way count: a program that leaves them out, or rounds other values in their place, can miss the bound.
Values may be sent and summed in bfloat16 or wider, within the bound.
A program may use at most 192 MiB of HBM per device.

```python
import math
import jax
import jax.numpy as jnp
from jax import lax

D = 3072
H = 48
HD = 64
SEGS = 4
HOME = 1024
PACK = 1280
TOTAL = 16384
N_DP = 16
N_BAG = 8


def packing(key):
    folded = jax.random.fold_in(key, 7001)
    subkeys = jax.random.split(folded, 7)
    unit_rows = HOME // N_DP
    half_unit = unit_rows // 2
    pair_count = N_DP // 2
    bag_order = jax.random.permutation(subkeys[0], N_DP)
    home_orders = jax.vmap(lambda subkey: jax.random.permutation(subkey, N_DP))(jax.random.split(subkeys[1], pair_count))
    home_ranks = jnp.argsort(home_orders, axis=1)
    tilt_signs = jax.random.randint(subkeys[2], (pair_count, N_DP), -1, 2)
    tilt_signs = tilt_signs.at[0].set(1)
    chosen = (home_ranks < N_DP // 2).astype(jnp.int32)
    tilt_rows = tilt_signs * chosen
    spare_rows = jax.random.randint(subkeys[3], (pair_count, N_DP), 0, half_unit + 1)
    leader = home_orders[0, 0]
    spare_rows = spare_rows.at[0, leader].set(half_unit).at[0, (leader + 1) % N_DP].set(0)
    swing_rows = half_unit * tilt_rows + spare_rows - jnp.roll(spare_rows, -1, axis=1)
    counts = jnp.zeros((N_DP, N_DP), jnp.int32)
    counts = counts.at[:, bag_order[0::2]].set((unit_rows + swing_rows).T)
    counts = counts.at[:, bag_order[1::2]].set((unit_rows - swing_rows).T)
    bag_fills = jnp.sum(counts, axis=0)
    inclusive = jnp.cumsum(counts, axis=1)
    ahead_rows = jnp.cumsum(counts, axis=0) - counts
    row_ids = jnp.arange(HOME, dtype=jnp.int32)
    row_bag = jnp.sum((row_ids[None, :, None] >= inclusive[:, None, :]).astype(jnp.int32), axis=2)
    run_begin = jnp.take_along_axis(inclusive - counts, row_bag, axis=1)
    within = row_ids[None, :] - run_begin
    incoming = jnp.take_along_axis(ahead_rows, row_bag, axis=1) + within
    slot_ids = jnp.arange(PACK, dtype=jnp.int32)[None, :]
    slot_keys = jax.random.randint(subkeys[4], (N_DP, PACK), 0, 2 ** 16) * PACK + slot_ids
    slot_keys = slot_keys + (slot_ids >= bag_fills[:, None]).astype(jnp.int32) * 2 ** 29
    slot_order = jnp.argsort(slot_keys, axis=1).astype(jnp.int32)
    row_slot = slot_order[row_bag, incoming]
    row_value = row_bag * PACK + row_slot
    shuffle = jax.vmap(lambda subkey: jax.random.permutation(subkey, HOME))(jax.random.split(subkeys[5], N_DP))
    plan_rows = jax.vmap(lambda values_in, shuffle_order: jnp.zeros((HOME,), jnp.int32).at[shuffle_order].set(values_in))(row_value, shuffle)
    plan_rows = plan_rows.reshape(N_DP * HOME).astype(jnp.int32)
    cut_points = jax.random.randint(subkeys[6], (N_DP, SEGS - 1), 1, jnp.maximum(bag_fills, 2)[:, None])
    is_full = jnp.arange(N_DP) == bag_order[0]
    cut_points = jnp.where(is_full[:, None], bag_fills[:, None], cut_points)
    cut_points = jnp.sort(cut_points, axis=1)
    bounds = jnp.concatenate([jnp.zeros((N_DP, 1), jnp.int32), cut_points.astype(jnp.int32), bag_fills[:, None].astype(jnp.int32)], axis=1)
    length_list = (bounds[:, 1:] - bounds[:, :-1]).astype(jnp.int32)
    return (plan_rows, length_list)


def draw_row_plan(key, part):
    return packing(key)[0]


def draw_sample_lengths(key, part):
    return packing(key)[1]


def draw_qkv_weight(key, part):
    folded = jax.random.fold_in(key, 7101)
    normals = jnp.clip(jax.random.normal(folded, (3, D, H * HD), jnp.float32), -4.0, 4.0) * D ** (-0.5)
    return normals.astype(jnp.bfloat16)


def draw_norm_gain(key, part):
    folded = jax.random.fold_in(key, 7201)
    subkeys = jax.random.split(folded, 1)
    element = jnp.exp(jax.random.uniform(subkeys[0], (2, H * HD), jnp.float32, 0.0, math.log(3.0)))
    return element


def place_ends(array, own_key, smallest, top_value):
    index_at = [jax.random.randint(jax.random.fold_in(own_key, axis), (), 0, length) for axis, length in enumerate(array.shape)]
    widest = array.shape.index(max(array.shape))
    beside = index_at[:widest] + [(index_at[widest] + 1) % array.shape[widest]] + index_at[widest + 1:]
    return array.at[tuple(index_at)].set(smallest).at[tuple(beside)].set(top_value)


def steps_of(key, shape, pieces, smallest, high):
    def one(position, parts):
        heights = jax.random.uniform(jax.random.fold_in(jax.random.fold_in(key, 6), position), (parts,), jnp.float32, smallest / len(pieces), high / len(pieces))
        return jnp.repeat(jnp.exp(heights), shape[position] // parts).reshape((-1,) + (1,) * (len(shape) - position - 1))

    loudness = one(*pieces[0])
    for cut in pieces[1:]:
        loudness = loudness * one(*cut)
    return loudness


def scatter_about(rng, shape, scale, reach, cuts=(), held_as=jnp.bfloat16):
    entries = scale * jax.random.normal(rng, shape, jnp.float32)
    if cuts:
        entries = entries * steps_of(rng, shape, cuts, -0.22, 0.18)
    return jnp.clip(entries, -reach, reach).astype(held_as)


def setup_inputs(seed: int = 0) -> dict:
    splits = jax.random.split(jax.random.key(seed), 9)
    return {
        "home_tokens": scatter_about(splits[0], (TOTAL, D), 1.0, 6.0, ((0, 16), (1, 8))),
        "mod_weight": scatter_about(splits[1], (2, D, D), D ** -0.5, 0.109375, ((2, 8),)),
        "qkv_weight": draw_qkv_weight(jax.random.fold_in(splits[8], 71), 0),
        "norm_gain": draw_norm_gain(jax.random.fold_in(splits[8], 71), 0),
        "output_weight": scatter_about(splits[4], (H * HD, D), (H * HD) ** -0.5, 0.109375, ((0, 8),)),
        "row_plan": draw_row_plan(jax.random.fold_in(splits[8], 71), 0),
        "sample_lengths": draw_sample_lengths(jax.random.fold_in(splits[8], 71), 0),
        "modality": place_ends(jax.random.randint(splits[7], (N_DP, SEGS), 0, 2), jax.random.fold_in(splits[7], 1), 0, 1).astype(jnp.int32),
    }


epsilon = 1e-06

def head_norm(heads_in, gains):
    centre = lax.optimization_barrier(jnp.mean(heads_in, axis=-1, keepdims=True))
    shifted = heads_in - centre
    spread = lax.optimization_barrier(jnp.mean(shifted * shifted, axis=-1, keepdims=True))
    return shifted * lax.rsqrt(spread + epsilon) * gains

def reference(home_tokens, mod_weight, qkv_weight, norm_gain, output_weight, row_plan, sample_lengths, modality):
    sample_ends = jnp.cumsum(sample_lengths, axis=1).astype(jnp.int32)
    bag_of = (row_plan // PACK).astype(jnp.int32)
    slot_of = (row_plan % PACK).astype(jnp.int32)
    row_ends = sample_ends[bag_of]
    row_sample = lax.optimization_barrier(jnp.sum((slot_of[:, None] >= row_ends).astype(jnp.int32), axis=1))
    row_modality = modality[bag_of, row_sample]
    leading_product = jnp.dot(home_tokens, mod_weight[0], preferred_element_type=jnp.float32)
    second_product = jnp.dot(home_tokens, mod_weight[1], preferred_element_type=jnp.float32)
    projected = jnp.where(row_modality[:, None] == 0, leading_product, second_product).astype(jnp.bfloat16)
    packed = jnp.zeros((N_DP * PACK, D), jnp.bfloat16).at[row_plan].set(projected)
    group_heads = H // N_BAG
    group_width = group_heads * HD
    slot_ids = jnp.arange(PACK, dtype=jnp.int32)

    def one_bag(bag_index):
        bag_rows = lax.dynamic_slice_in_dim(packed, (bag_index * PACK).astype(jnp.int32), PACK, 0)
        bag_ends = lax.dynamic_index_in_dim(sample_ends, bag_index, 0, keepdims=False)
        sample_ids = lax.optimization_barrier(jnp.sum((slot_ids[:, None] >= bag_ends[None, :]).astype(jnp.int32), axis=1))
        allowed = sample_ids[:, None] == sample_ids[None, :]

        def one_group(group_index):
            offset = (group_index * group_width).astype(jnp.int32)
            weights = lax.dynamic_slice_in_dim(qkv_weight, offset, group_width, 2)
            gains = lax.dynamic_slice_in_dim(norm_gain, offset, group_width, 1)
            queries = jnp.dot(bag_rows, weights[0], preferred_element_type=jnp.float32)
            keys_raw = jnp.dot(bag_rows, weights[1], preferred_element_type=jnp.float32)
            values = jnp.dot(bag_rows, weights[2], preferred_element_type=jnp.float32)
            queries = head_norm(queries.reshape(PACK, group_heads, HD), gains[0].reshape(group_heads, HD)).astype(jnp.bfloat16)
            keys_normed = head_norm(keys_raw.reshape(PACK, group_heads, HD), gains[1].reshape(group_heads, HD)).astype(jnp.bfloat16)
            values = values.astype(jnp.bfloat16).reshape(PACK, group_heads, HD)
            scores = jnp.einsum('qhd,khd->hqk', queries.astype(jnp.float32), keys_normed.astype(jnp.float32)) * HD ** (-0.5)
            scores = jnp.where(allowed[None], scores, -jnp.inf)
            row_max = lax.optimization_barrier(jnp.max(scores, axis=2, keepdims=True))
            raised = jnp.exp(scores - row_max)
            weights_soft = (raised / lax.optimization_barrier(jnp.sum(raised, axis=2, keepdims=True))).astype(jnp.bfloat16)
            attended = jnp.einsum('hqk,khd->qhd', weights_soft.astype(jnp.float32), values.astype(jnp.float32))
            attended = attended.astype(jnp.bfloat16).reshape(PACK, group_width)
            out_rows = lax.dynamic_slice_in_dim(output_weight, offset, group_width, 0)
            partial_value = jnp.dot(attended, out_rows, preferred_element_type=jnp.float32).astype(jnp.bfloat16)
            return lax.optimization_barrier(partial_value).astype(jnp.float32)
        return lax.optimization_barrier(jnp.sum(lax.map(one_group, jnp.arange(N_BAG, dtype=jnp.int32)), axis=0))
    summed = lax.map(one_bag, jnp.arange(N_DP, dtype=jnp.int32)).reshape(N_DP * PACK, D)
    return summed[row_plan].astype(jnp.bfloat16)
```

```python
import functools

import jax
import jax.numpy as jnp
from jax import lax
from jax.experimental import pallas as pl
from jax.experimental.pallas import tpu as pltpu
from jax.sharding import PartitionSpec as P

HD = 64
EPS = 1e-06
LOG2E = 1.4426950408889634


def head_norm(heads_in, gains):
    centre = jnp.mean(heads_in, axis=-1, keepdims=True)
    shifted = heads_in - centre
    spread = jnp.mean(shifted * shifted, axis=-1, keepdims=True)
    return shifted * lax.rsqrt(spread + EPS) * gains


def attention_kernel(q_ref, k_ref, v_ref, sq_ref, sk_ref, o_ref):
    def extend(x, sample, keep_low, fill):
        lane = lax.broadcasted_iota(jnp.int32, x.shape, 1)
        low = lane < HD
        hit = (lane % HD) == sample
        return jnp.where(low == keep_low, x, jnp.where(hit, fill, 0.0).astype(x.dtype))

    q, k, v = q_ref[...], k_ref[...], v_ref[...]
    lane_v = lax.broadcasted_iota(jnp.int32, v.shape, 1)
    outs = []
    for keep_low in (True, False):
        qx = extend(q, sq_ref[...], keep_low, 128.0)
        kx = extend(k, sk_ref[...], keep_low, 128.0)
        vx = jnp.where((lane_v < HD) == keep_low, v, jnp.ones_like(v))
        s = lax.dot_general(qx, kx, (((1,), (1,)), ((), ())), preferred_element_type=jnp.float32)
        m = jnp.max(s, axis=1, keepdims=True)
        p = jnp.exp2((s - m) * (LOG2E * HD ** -0.5)).astype(jnp.bfloat16)
        o = jnp.dot(p, vx, preferred_element_type=jnp.float32)
        outs.append(o / pltpu.roll(o, HD, 1))
    lane_o = lax.broadcasted_iota(jnp.int32, outs[0].shape, 1)
    o_ref[...] = jnp.where(lane_o < HD, outs[0], outs[1]).astype(o_ref.dtype)


def attention(q, k, v, sample_col):
    rows, width = q.shape
    bq = rows // 5
    return pl.pallas_call(
        attention_kernel,
        grid=(width // 128, rows // bq),
        in_specs=[
            pl.BlockSpec((bq, 128), lambda h, i: (i, h)),
            pl.BlockSpec((rows, 128), lambda h, i: (0, h)),
            pl.BlockSpec((rows, 128), lambda h, i: (0, h)),
            pl.BlockSpec((bq, 1), lambda h, i: (i, 0)),
            pl.BlockSpec((rows, 1), lambda h, i: (0, 0)),
        ],
        out_specs=pl.BlockSpec((bq, 128), lambda h, i: (i, h)),
        out_shape=jax.ShapeDtypeStruct((rows, width), jnp.bfloat16),
    )(q, k, v, sample_col, sample_col)


def plan_tables(row_plan, sample_lengths, modality, my_home, homes, resident, pack):
    cap = 2 * resident // homes
    dest = row_plan.reshape(homes, resident)
    bag = dest // pack
    slot = dest % pack
    bag_ids = jnp.arange(homes, dtype=jnp.int32)
    onehot = (bag[:, :, None] == bag_ids).astype(jnp.bfloat16)
    row_ids = jnp.arange(resident, dtype=jnp.int32)
    lower = (row_ids[:, None] > row_ids[None, :]).astype(jnp.bfloat16)
    ahead = jnp.einsum("mt,pta->pma", lower, onehot, preferred_element_type=jnp.float32)
    position = jnp.sum(ahead * onehot.astype(jnp.float32), axis=2).astype(jnp.int32)
    key = jnp.where(bag == my_home, position, -1)
    cap_ids = jnp.arange(cap, dtype=jnp.int32)
    slot_table = jnp.sum(
        jnp.where(key[:, None, :] == cap_ids[None, :, None], slot[:, None, :] + 1, 0), axis=2
    ).reshape(homes * cap) - 1
    own_bag = lax.dynamic_index_in_dim(bag, my_home, 0, keepdims=False)
    own_slot = lax.dynamic_index_in_dim(slot, my_home, 0, keepdims=False)
    own_index = own_bag * cap + lax.dynamic_index_in_dim(position, my_home, 0, keepdims=False)
    ends = jnp.cumsum(sample_lengths, axis=1)
    hits = (own_bag[:, None] == bag_ids[None, :])[:, :, None]
    row_ends = jnp.sum(jnp.where(hits, ends[None], 0), axis=1)
    row_mods = jnp.sum(jnp.where(hits, modality[None], 0), axis=1)
    row_sample = jnp.sum((own_slot[:, None] >= row_ends).astype(jnp.int32), axis=1)
    pick = row_sample[:, None] == jnp.arange(ends.shape[1], dtype=jnp.int32)[None, :]
    row_modality = jnp.sum(jnp.where(pick, row_mods, 0), axis=1)
    my_ends = jnp.sum(jnp.where((bag_ids == my_home)[:, None], ends, 0), axis=0)
    slot_ids = jnp.arange(pack, dtype=jnp.int32)
    sample_ids = jnp.sum((slot_ids[:, None] >= my_ends[None, :]).astype(jnp.int32), axis=1)
    return own_index, slot_table, row_modality, sample_ids


def pick_rows(left, right, rows):
    hot = (left == right).astype(jnp.bfloat16)
    return jnp.dot(hot, rows, preferred_element_type=jnp.float32).astype(jnp.bfloat16)


def body(
    home_tokens,
    mod_weight,
    qkv_weight,
    norm_gain,
    output_weight,
    row_plan,
    sample_lengths,
    modality,
):
    homes = lax.axis_size("dp")
    members = lax.axis_size("bag")
    my_home = lax.axis_index("dp")
    resident, part = home_tokens.shape
    pack = resident + resident // 4
    cap = 2 * resident // homes
    slots = cap * homes
    heads = part // HD
    own_index, slot_table, row_modality, sample_ids = plan_tables(
        row_plan, sample_lengths, modality, my_home, homes, resident, pack
    )
    slot_ids = jnp.arange(slots, dtype=jnp.int32)
    pack_ids = jnp.arange(pack, dtype=jnp.int32)
    weight_blocks = lax.all_to_all(
        output_weight.reshape(part, members, part), "bag", split_axis=1, concat_axis=0
    )
    tokens = lax.all_gather(home_tokens, "bag", axis=1, tiled=True)
    is_first = (row_modality == 0)[:, None]
    blank = jnp.zeros_like(tokens)
    projected = (
        jnp.dot(jnp.where(is_first, tokens, blank), mod_weight[0], preferred_element_type=jnp.float32)
        + jnp.dot(jnp.where(is_first, blank, tokens), mod_weight[1], preferred_element_type=jnp.float32)
    ).astype(jnp.bfloat16)
    outgoing = pick_rows(slot_ids[:, None], own_index[None, :], projected)
    arrived = lax.all_to_all(
        outgoing.reshape(homes, cap, part), "dp", split_axis=0, concat_axis=0, tiled=True
    ).reshape(slots, part)
    packed_part = pick_rows(pack_ids[:, None], slot_table[None, :], arrived)
    packed = lax.all_gather(packed_part, "bag", axis=1, tiled=True)
    stacked = jnp.einsum("pd,kdh->kph", packed, qkv_weight, preferred_element_type=jnp.float32)
    queries = head_norm(
        stacked[0].reshape(pack, heads, HD), norm_gain[0].reshape(heads, HD)
    ).astype(jnp.bfloat16).reshape(pack, part)
    keys = head_norm(
        stacked[1].reshape(pack, heads, HD), norm_gain[1].reshape(heads, HD)
    ).astype(jnp.bfloat16).reshape(pack, part)
    values = stacked[2].astype(jnp.bfloat16)
    attended = attention(queries, keys, values, sample_ids[:, None])
    back = pick_rows(slot_table[:, None], pack_ids[None, :], attended)
    returned = lax.all_to_all(
        back.reshape(homes, cap, part), "dp", split_axis=0, concat_axis=0, tiled=True
    ).reshape(slots, part)
    home_part = pick_rows(own_index[:, None], slot_ids[None, :], returned)
    home_rows = lax.all_gather(home_part, "bag", axis=0)
    partial = jnp.einsum(
        "gra,gab->grb", home_rows, weight_blocks.reshape(members, part, part), preferred_element_type=jnp.float32
    ).astype(jnp.bfloat16)
    return jnp.sum(partial.astype(jnp.float32), axis=0).astype(jnp.bfloat16)


def solution(mesh):
    in_specs = (
        P("dp", "bag"),
        P(None, None, "bag"),
        P(None, None, "bag"),
        P(None, "bag"),
        P("bag", None),
        P(),
        P(),
        P(),
    )
    return jax.shard_map(body, mesh=mesh, in_specs=in_specs, out_specs=P("dp", "bag"), check_vma=False)
```

```python
import functools

import jax
import jax.numpy as jnp
from jax import lax
from jax.experimental import pallas as pl
from jax.experimental.pallas import tpu as pltpu
from jax.sharding import PartitionSpec as P

HD = 64
EPS = 1e-06
LOG2E = 1.4426950408889634


def plan_tables(row_plan, sample_lengths, modality, my_home, homes, resident, pack):
    cap = 2 * resident // homes
    dest = row_plan.reshape(homes, resident)
    bag = dest // pack
    slot = dest % pack
    bag_ids = jnp.arange(homes, dtype=jnp.int32)
    onehot = (bag[:, :, None] == bag_ids).astype(jnp.bfloat16)
    row_ids = jnp.arange(resident, dtype=jnp.int32)
    lower = (row_ids[:, None] > row_ids[None, :]).astype(jnp.bfloat16)
    ahead = jnp.einsum("mt,pta->pma", lower, onehot, preferred_element_type=jnp.float32)
    position = jnp.sum(ahead * onehot.astype(jnp.float32), axis=2).astype(jnp.int32)
    key = jnp.where(bag == my_home, position, -1)
    cap_ids = jnp.arange(cap, dtype=jnp.int32)
    slot_table = jnp.sum(
        jnp.where(key[:, None, :] == cap_ids[None, :, None], slot[:, None, :] + 1, 0), axis=2
    ).reshape(homes * cap) - 1
    own_bag = lax.dynamic_index_in_dim(bag, my_home, 0, keepdims=False)
    own_slot = lax.dynamic_index_in_dim(slot, my_home, 0, keepdims=False)
    own_index = own_bag * cap + lax.dynamic_index_in_dim(position, my_home, 0, keepdims=False)
    ends = jnp.cumsum(sample_lengths, axis=1)
    hits = (own_bag[:, None] == bag_ids[None, :])[:, :, None]
    row_ends = jnp.sum(jnp.where(hits, ends[None], 0), axis=1)
    row_mods = jnp.sum(jnp.where(hits, modality[None], 0), axis=1)
    row_sample = jnp.sum((own_slot[:, None] >= row_ends).astype(jnp.int32), axis=1)
    pick = row_sample[:, None] == jnp.arange(ends.shape[1], dtype=jnp.int32)[None, :]
    row_modality = jnp.sum(jnp.where(pick, row_mods, 0), axis=1)
    my_ends = jnp.sum(jnp.where((bag_ids == my_home)[:, None], ends, 0), axis=0)
    slot_ids = jnp.arange(pack, dtype=jnp.int32)
    sample_ids = jnp.sum((slot_ids[:, None] >= my_ends[None, :]).astype(jnp.int32), axis=1)
    return own_index, slot_table, row_modality, sample_ids


MESH = pl.DeviceIdType.MESH
LANES = 128


def remote(src, dst, send_sem, recv_sem, where):
    return pltpu.make_async_remote_copy(
        src_ref=src, dst_ref=dst, send_sem=send_sem, recv_sem=recv_sem, device_id=where, device_id_type=MESH
    )


def gather_z(first, buf, send_sems, recv_sems, near, far, twin, on_ready):
    rows, width = buf.shape[1] // 2, buf.shape[2] // 2
    sent = []
    lands = {}

    def view(k, lane, half):
        return buf.at[k, pl.ds(half * rows, rows), pl.ds(lane * width, width)]

    def send(source, half, k, lane, where):
        copy = remote(source, view(k, lane, half), send_sems.at[len(sent)], recv_sems.at[k, lane, half], where)
        copy.start()
        sent.append(copy)
        lands[k, lane, half] = copy

    send(first(0), 0, 3, 0, near)
    send(first(1), 1, 1, 0, far)
    send(first(0), 0, 0, 1, twin)
    send(first(1), 1, 0, 1, twin)
    send(first(1), 1, 3, 0, near)
    send(first(0), 0, 1, 0, far)
    for half in (0, 1):
        lands[0, 1, half].wait_recv()
        on_ready(0, half)
    lands[3, 0, 0].wait_recv()
    send(view(3, 0, 0), 0, 2, 0, near)
    send(view(3, 0, 0), 0, 3, 1, twin)
    lands[1, 0, 1].wait_recv()
    send(view(1, 0, 1), 1, 2, 0, far)
    send(view(1, 0, 1), 1, 1, 1, twin)
    for pairs in (((3, 0), (1, 1)), ((3, 1), (1, 0)), ((2, 0), (2, 1))):
        for k, half in pairs:
            if (k, half) not in ((3, 0), (1, 1)):
                lands[k, 0, half].wait_recv()
                send(view(k, 0, half), half, k, 1, twin)
        for k, half in pairs:
            lands[k, 1, half].wait_recv()
            on_ready(k, half)
    for copy in sent:
        copy.wait_send()


def head_scale(x, gain):
    low = lax.broadcasted_iota(jnp.int32, x.shape, 1) < HD

    def mean(t):
        left = jnp.sum(jnp.where(low, t, 0.0), axis=1, keepdims=True)
        right = jnp.sum(jnp.where(low, 0.0, t), axis=1, keepdims=True)
        return jnp.where(low, left, right) * (1.0 / HD)

    shifted = x - mean(x)
    return (shifted * lax.rsqrt(mean(shifted * shifted) + EPS) * gain).astype(jnp.bfloat16)


def extend(x, sample, keep_low):
    lane = lax.broadcasted_iota(jnp.int32, x.shape, 1)
    mark = jnp.where((lane % HD) == sample, 128.0, 0.0).astype(x.dtype)
    return jnp.where((lane < HD) == keep_low, x, mark)


def mega_kernel(
    homes_x, homes_y,
    tokens, modw, qkvw, outw, gain, own_row, table, cols,
    out,
    buf1, w1, acc1, proj, sbuf, abuf, buf2, w2, acc2, acc_pack, kx, vx, att, buf3, w3, acc3,
    sem_w1, sem_w2, sem_w3s, sem_w3r, sem_own,
    s1, r1, s2, r2, s3, r3, sa, ra, sb, rb,
):
    homes = homes_x * homes_y
    me = lax.axis_index("dp")
    bag = lax.axis_index("bag")
    x, y = lax.div(me, homes_y), lax.rem(me, homes_y)
    z, core = lax.div(bag, 2), lax.rem(bag, 2)
    resident, part = tokens.shape
    pack = buf2.shape[1]
    cap = sbuf.shape[1]

    def member(k, lane):
        return lax.rem(z + k, 4) * 2 + (core if lane == 0 else 1 - core)

    def home(step, sign):
        dx, dy = step // homes_y, step % homes_y
        if sign < 0:
            dx, dy = homes_x - dx, homes_y - dy
        return lax.rem(x + dx, homes_x) * homes_y + lax.rem(y + dy, homes_y)

    near, far, twin = {"bag": member(1, 0)}, {"bag": member(3, 0)}, {"bag": member(0, 1)}

    def rows_of(index):
        return pl.ds(pl.multiple_of(index * part, part), part)

    w1_loads, w2_loads = [], []
    for k in (0, 3, 1, 2):
        for lane in (0, 1):
            at = (k * 2 + lane) * part
            for m in range(2):
                w1_loads.append(pltpu.make_async_copy(
                    modw.at[m, rows_of(member(k, lane)), :],
                    w1.at[pl.ds(at, part), pl.ds(m * part, part)], sem_w1.at[len(w1_loads)]))
            for m in range(3):
                w2_loads.append(pltpu.make_async_copy(
                    qkvw.at[m, rows_of(member(k, lane)), :],
                    w2.at[pl.ds(at, part), pl.ds(m * part, part)], sem_w2.at[len(w2_loads)]))
    own_load = pltpu.make_async_copy(tokens, buf1.at[0, :, pl.ds(0, part)], sem_own.at[0])
    own_load.start()
    for load in w1_loads:
        load.start()

    barrier = pltpu.get_barrier_semaphore()
    for step in range(1, homes):
        pl.semaphore_signal(barrier, inc=1, device_id={"dp": home(step, 1)}, device_id_type=MESH)
    for step in range(1, 8):
        pl.semaphore_signal(barrier, inc=1, device_id={"bag": lax.rem(bag + step, 8)}, device_id_type=MESH)
    pl.semaphore_wait(barrier, homes - 1 + 7)

    own_load.wait()

    half1 = resident // 2

    def project(k, half):
        if (k, half) == (0, 0):
            for load in w1_loads:
                load.wait()
            for load in w2_loads:
                load.start()
        rows = pl.ds(half * half1, half1)
        value = jnp.dot(
            buf1[k, rows, :], w1[pl.ds(k * 2 * part, 2 * part), :], preferred_element_type=jnp.float32)
        if k == 0:
            acc1[rows, :] = value
        else:
            acc1[rows, :] += value

    gather_z(lambda half: buf1.at[0, pl.ds(half * half1, half1), pl.ds(0, part)],
             buf1, s1, r1, near, far, twin, project)
    is_first = cols[pl.ds(0, resident), 2:3] == 0
    proj[...] = jnp.where(is_first, acc1[:, :part], acc1[:, part:]).astype(jnp.bfloat16)

    order = sorted(range(1, homes), key=lambda s: -(min(s // homes_y, homes_x - s // homes_y)
                                                    + min(s % homes_y, homes_y - s % homes_y))) + [0]

    copies = {}
    for step in order:
        ids = lax.broadcasted_iota(jnp.int32, (cap, resident), 0) + home(step, 1) * cap
        hot = (own_row[...] == ids).astype(jnp.bfloat16)
        block = jnp.dot(hot, proj[...], preferred_element_type=jnp.float32).astype(jnp.bfloat16)
        if step:
            sbuf[step] = block
            copies[step] = remote(sbuf.at[step], abuf.at[step], sa.at[step], ra.at[step], {"dp": home(step, 1)})
            copies[step].start()
        else:
            abuf[0] = block
    group = 4
    arrival = [0] + order[:-1]
    for start in range(0, homes, group):
        steps = arrival[start:start + group]
        pieces, rows = [], []
        for step in steps:
            if step:
                copies[step].wait_recv()
            ids = lax.broadcasted_iota(jnp.int32, (pack, cap), 0)
            pieces.append((ids == table[pl.ds(home(step, -1), 1), :]).astype(jnp.bfloat16))
            rows.append(abuf[step])
        value = jnp.dot(jnp.concatenate(pieces, axis=1), jnp.concatenate(rows, axis=0),
                        preferred_element_type=jnp.float32)
        if start == 0:
            acc_pack[...] = value
        elif start + group < homes:
            acc_pack[...] += value
        else:
            buf2[0, :, 0:part] = (acc_pack[...] + value).astype(jnp.bfloat16)
    for step in order[:-1]:
        copies[step].wait_send()

    half2 = pack // 2

    def qkv(k, half):
        if (k, half) == (0, 0):
            for load in w2_loads:
                load.wait()
        rows = pl.ds(half * half2, half2)
        value = jnp.dot(
            buf2[k, rows, :], w2[pl.ds(k * 2 * part, 2 * part), :], preferred_element_type=jnp.float32)
        if k == 0:
            acc2[rows, :] = value
        else:
            acc2[rows, :] += value

    gather_z(lambda half: buf2.at[0, pl.ds(half * half2, half2), pl.ds(0, part)],
             buf2, s2, r2, near, far, twin, qkv)

    w3_copies = []
    w3_own = pltpu.make_async_copy(
        outw.at[:, rows_of(bag)], w3.at[pl.ds(0, part), :], sem_own.at[1])
    w3_own.start()
    for k in range(4):
        for lane in range(2):
            if k or lane:
                target = lax.rem(z + 4 - k, 4) * 2 + (core if lane == 0 else 1 - core)
                index = k * 2 + lane
                copy = remote(outw.at[:, rows_of(target)], w3.at[pl.ds(index * part, part), :],
                              sem_w3s.at[index], sem_w3r.at[index], {"bag": target})
                copy.start()
                w3_copies.append(copy)

    block_rows = pack // 5
    for pair in range(part // LANES):
        lanes = pl.ds(pair * LANES, LANES)
        key = head_scale(acc2[:, pl.ds(part + pair * LANES, LANES)], gain[1:2, lanes])
        value = acc2[:, pl.ds(2 * part + pair * LANES, LANES)].astype(jnp.bfloat16)
        low = lax.broadcasted_iota(jnp.int32, value.shape, 1) < HD
        for head in range(2):
            kx[head] = extend(key, cols[pl.ds(0, pack), 3:4], head == 0)
            vx[head] = jnp.where(low == (head == 0), value, jnp.ones_like(value))

        def attend(index, carry):
            rows = pl.ds(pl.multiple_of(index * block_rows, block_rows), block_rows)
            query = head_scale(acc2[rows, lanes], gain[0:1, lanes])
            results = []
            for head in range(2):
                qx = extend(query, cols[rows, 3:4], head == 0)
                s = lax.dot_general(qx, kx[head], (((1,), (1,)), ((), ())), preferred_element_type=jnp.float32)
                top = jnp.max(s, axis=1, keepdims=True)
                p = jnp.exp2((s - top) * (LOG2E * HD ** -0.5)).astype(jnp.bfloat16)
                o = jnp.dot(p, vx[head], preferred_element_type=jnp.float32)
                results.append(o / pltpu.roll(o, HD, 1))
            low_out = lax.broadcasted_iota(jnp.int32, results[0].shape, 1) < HD
            att[rows, lanes] = jnp.where(low_out, results[0], results[1]).astype(jnp.bfloat16)
            return carry

        lax.fori_loop(0, 5, attend, 0)

    copies = {}
    for step in order:
        ids = lax.broadcasted_iota(jnp.int32, (cap, pack), 1)
        begin = pl.multiple_of(home(step, 1) * cap, cap)
        hot = (cols[pl.ds(begin, cap), 0:1] == ids).astype(jnp.bfloat16)
        block = jnp.dot(hot, att[...], preferred_element_type=jnp.float32).astype(jnp.bfloat16)
        if step:
            sbuf[step] = block
            copies[step] = remote(sbuf.at[step], abuf.at[homes + step], sb.at[step], rb.at[step],
                                  {"dp": home(step, 1)})
            copies[step].start()
        else:
            abuf[homes] = block
    for start in range(0, homes, group):
        steps = arrival[start:start + group]
        pieces, rows = [], []
        for step in steps:
            if step:
                copies[step].wait_recv()
            ids = lax.broadcasted_iota(jnp.int32, (resident, cap), 1) + home(step, -1) * cap
            pieces.append((ids == cols[pl.ds(0, resident), 1:2]).astype(jnp.bfloat16))
            rows.append(abuf[homes + step])
        value = jnp.dot(jnp.concatenate(pieces, axis=1), jnp.concatenate(rows, axis=0),
                        preferred_element_type=jnp.float32)
        if start == 0:
            acc3[...] = value
        elif start + group < homes:
            acc3[...] += value
        else:
            buf3[0, :, 0:part] = (acc3[...] + value).astype(jnp.bfloat16)
    for step in order[:-1]:
        copies[step].wait_send()

    w3_own.wait()
    for copy in w3_copies:
        copy.wait()

    def finish(k, half):
        rows = pl.ds(half * half1, half1)
        value = jnp.dot(
            buf3[k, rows, :], w3[pl.ds(k * 2 * part, 2 * part), :], preferred_element_type=jnp.float32)
        if k == 0:
            acc3[rows, :] = value
        elif k == 2:
            out[rows, :] = (acc3[rows, :] + value).astype(jnp.bfloat16)
        else:
            acc3[rows, :] += value

    gather_z(lambda half: buf3.at[0, pl.ds(half * half1, half1), pl.ds(0, part)],
             buf3, s3, r3, near, far, twin, finish)


def body(
    home_tokens,
    mod_weight,
    qkv_weight,
    norm_gain,
    output_weight,
    row_plan,
    sample_lengths,
    modality,
):
    homes = lax.axis_size("dp")
    my_home = lax.axis_index("dp")
    resident, part = home_tokens.shape
    full = mod_weight.shape[1]
    pack = resident + resident // 4
    cap = 2 * resident // homes
    slots = cap * homes
    own_index, slot_table, row_modality, sample_ids = plan_tables(
        row_plan, sample_lengths, modality, my_home, homes, resident, pack
    )

    def pad(values):
        return jnp.pad(values, (0, slots - values.shape[0]))

    cols = jnp.stack([slot_table, pad(own_index), pad(row_modality), pad(sample_ids)], axis=1)
    bf16, f32 = jnp.bfloat16, jnp.float32
    any_spec = pl.BlockSpec(memory_space=pl.ANY)
    vmem = pl.BlockSpec(memory_space=pltpu.VMEM)
    dma = pltpu.SemaphoreType.DMA
    kernel = functools.partial(mega_kernel, 4, 4)
    return pl.pallas_call(
        kernel,
        out_shape=jax.ShapeDtypeStruct((resident, part), bf16),
        in_specs=[any_spec] * 4 + [vmem] * 4,
        out_specs=vmem,
        scratch_shapes=[
            pltpu.VMEM((4, resident, 2 * part), bf16),
            pltpu.VMEM((full, 2 * part), bf16),
            pltpu.VMEM((resident, 2 * part), f32),
            pltpu.VMEM((resident, part), bf16),
            pltpu.VMEM((homes, cap, part), bf16),
            pltpu.VMEM((2 * homes, cap, part), bf16),
            pltpu.VMEM((4, pack, 2 * part), bf16),
            pltpu.VMEM((full, 3 * part), bf16),
            pltpu.VMEM((pack, 3 * part), f32),
            pltpu.VMEM((pack, part), f32),
            pltpu.VMEM((2, pack, 128), bf16),
            pltpu.VMEM((2, pack, 128), bf16),
            pltpu.VMEM((pack, part), bf16),
            pltpu.VMEM((4, resident, 2 * part), bf16),
            pltpu.VMEM((full, part), bf16),
            pltpu.VMEM((resident, part), f32),
            dma((16,)), dma((24,)), dma((8,)), dma((8,)), dma((2,)),
            dma((14,)), dma((4, 2, 2)), dma((14,)), dma((4, 2, 2)), dma((14,)), dma((4, 2, 2)),
            dma((homes,)), dma((homes,)), dma((homes,)), dma((homes,)),
        ],
        compiler_params=pltpu.CompilerParams(
            collective_id=0, has_side_effects=True, vmem_limit_bytes=67043328),
        name="mega",
    )(
        home_tokens, mod_weight, qkv_weight, output_weight, norm_gain,
        own_index[None, :], slot_table.reshape(homes, cap), cols,
    )


def solution(mesh):
    in_specs = (
        P("dp", "bag"),
        P(None, None, "bag"),
        P(None, None, "bag"),
        P(None, "bag"),
        P("bag", None),
        P(),
        P(),
        P(),
    )
    return jax.shard_map(body, mesh=mesh, in_specs=in_specs, out_specs=P("dp", "bag"), check_vma=False)
```

```python
import functools

import jax
import jax.numpy as jnp
from jax import lax
from jax.experimental import pallas as pl
from jax.experimental.pallas import tpu as pltpu
from jax.sharding import PartitionSpec as P

HD = 64
EPS = 1e-06
LOG2E = 1.4426950408889634


def plan_tables(row_plan, sample_lengths, modality, my_home, homes, resident, pack):
    cap = 2 * resident // homes
    dest = row_plan.reshape(homes, resident)
    bag = dest // pack
    slot = dest % pack
    bag_ids = jnp.arange(homes, dtype=jnp.int32)
    onehot = (bag[:, :, None] == bag_ids).astype(jnp.bfloat16)
    row_ids = jnp.arange(resident, dtype=jnp.int32)
    lower = (row_ids[:, None] > row_ids[None, :]).astype(jnp.bfloat16)
    ahead = jnp.einsum("mt,pta->pma", lower, onehot, preferred_element_type=jnp.float32)
    position = jnp.sum(ahead * onehot.astype(jnp.float32), axis=2).astype(jnp.int32)
    key = jnp.where(bag == my_home, position, -1)
    cap_ids = jnp.arange(cap, dtype=jnp.int32)
    slot_table = jnp.sum(
        jnp.where(key[:, None, :] == cap_ids[None, :, None], slot[:, None, :] + 1, 0), axis=2
    ).reshape(homes * cap) - 1
    own_bag = lax.dynamic_index_in_dim(bag, my_home, 0, keepdims=False)
    own_slot = lax.dynamic_index_in_dim(slot, my_home, 0, keepdims=False)
    own_index = own_bag * cap + lax.dynamic_index_in_dim(position, my_home, 0, keepdims=False)
    ends = jnp.cumsum(sample_lengths, axis=1)
    hits = (own_bag[:, None] == bag_ids[None, :])[:, :, None]
    row_ends = jnp.sum(jnp.where(hits, ends[None], 0), axis=1)
    row_mods = jnp.sum(jnp.where(hits, modality[None], 0), axis=1)
    row_sample = jnp.sum((own_slot[:, None] >= row_ends).astype(jnp.int32), axis=1)
    pick = row_sample[:, None] == jnp.arange(ends.shape[1], dtype=jnp.int32)[None, :]
    row_modality = jnp.sum(jnp.where(pick, row_mods, 0), axis=1)
    my_ends = jnp.sum(jnp.where((bag_ids == my_home)[:, None], ends, 0), axis=0)
    slot_ids = jnp.arange(pack, dtype=jnp.int32)
    sample_ids = jnp.sum((slot_ids[:, None] >= my_ends[None, :]).astype(jnp.int32), axis=1)
    return own_index, slot_table, row_modality, sample_ids


MESH = pl.DeviceIdType.MESH
LANES = 128


def remote(src, dst, send_sem, recv_sem, where):
    return pltpu.make_async_remote_copy(
        src_ref=src, dst_ref=dst, send_sem=send_sem, recv_sem=recv_sem, device_id=where, device_id_type=MESH
    )


class Ring:
    def __init__(self, first, buf, send_sems, recv_sems, places, on_ready):
        self.first, self.buf, self.send_sems, self.recv_sems = first, buf, send_sems, recv_sems
        self.near, self.far, self.twin = places
        self.on_ready = on_ready
        self.half = buf.shape[1] // 2
        self.sent, self.lands = [], {}

    def rows(self, half):
        return pl.ds(half * self.half, self.half)

    def view(self, k, lane, half):
        return self.buf.at[k, self.rows(half), pl.ds(lane * LANES, LANES)]

    def send(self, source, half, k, lane, where):
        copy = remote(source, self.view(k, lane, half), self.send_sems.at[len(self.sent)],
                      self.recv_sems.at[k, lane, half], where)
        copy.start()
        self.sent.append(copy)
        self.lands[k, lane, half] = copy

    def start(self):
        self.send(self.first(0), 0, 3, 0, self.near)
        self.send(self.first(1), 1, 1, 0, self.far)
        self.send(self.first(0), 0, 0, 1, self.twin)
        self.send(self.first(1), 1, 0, 1, self.twin)
        self.send(self.first(1), 1, 3, 0, self.near)
        self.send(self.first(0), 0, 1, 0, self.far)

    def forward(self, k, half):
        self.lands[k, 0, half].wait_recv()
        self.send(self.view(k, 0, half), half, k, 1, self.twin)

    def ready(self, k):
        for half in (0, 1):
            self.lands[k, 1, half].wait_recv()
        self.on_ready(k)

    def relay(self):
        for k, half, where in ((3, 0, self.near), (1, 1, self.far)):
            self.lands[k, 0, half].wait_recv()
            self.send(self.view(k, 0, half), half, 2, 0, where)
            self.send(self.view(k, 0, half), half, k, 1, self.twin)

    def own(self):
        self.ready(0)

    def beside(self):
        self.forward(3, 1)
        self.forward(1, 0)
        self.ready(3)
        self.ready(1)

    def across(self):
        self.forward(2, 0)
        self.forward(2, 1)
        self.ready(2)

    def finish(self):
        for copy in self.sent:
            copy.wait_send()


def loop(begin, end, step):
    def run(index, carry):
        step(index)
        return carry

    lax.fori_loop(begin, end, run, 0)


def head_scale(x, gain):
    low = lax.broadcasted_iota(jnp.int32, x.shape, 1) < HD

    def mean(t):
        left = jnp.sum(jnp.where(low, t, 0.0), axis=1, keepdims=True)
        right = jnp.sum(jnp.where(low, 0.0, t), axis=1, keepdims=True)
        return jnp.where(low, left, right) * (1.0 / HD)

    shifted = x - mean(x)
    return (shifted * lax.rsqrt(mean(shifted * shifted) + EPS) * gain).astype(jnp.bfloat16)


def extend(x, sample, keep_low):
    lane = lax.broadcasted_iota(jnp.int32, x.shape, 1)
    mark = jnp.where((lane % HD) == sample, 128.0, 0.0).astype(x.dtype)
    return jnp.where((lane < HD) == keep_low, x, mark)


def mega_kernel(
    homes_x, homes_y,
    tokens, modw, qkvw, outw, gain, own_row, table, cols,
    out,
    buf1, w1, acc1, proj, sbuf, abuf, buf2, w2, acc2, acc_pick, hots, kx, vx, att, back, buf3, w3, acc3,
    sem_w1, sem_w2, sem_w3s, sem_w3r, sem_own,
    s1, r1, s2, r2, s3, r3, sa, ra, sb, rb,
):
    homes = homes_x * homes_y
    me = lax.axis_index("dp")
    bag = lax.axis_index("bag")
    x, y = lax.div(me, homes_y), lax.rem(me, homes_y)
    z, core = lax.div(bag, 2), lax.rem(bag, 2)
    resident, part = tokens.shape
    pack = buf2.shape[2]
    cap = sbuf.shape[2]
    chunks = part // LANES
    f32, bf16 = jnp.float32, jnp.bfloat16

    def member(k, lane):
        return lax.rem(z + k, 4) * 2 + (core if lane == 0 else 1 - core)

    def home(turn, sign):
        step = lax.rem(turn * 5, homes)
        dx, dy = lax.div(step, homes_y), lax.rem(step, homes_y)
        if sign < 0:
            dx, dy = homes_x - dx, homes_y - dy
        return lax.rem(x + dx, homes_x) * homes_y + lax.rem(y + dy, homes_y)

    places = ({"bag": member(1, 0)}, {"bag": member(3, 0)}, {"bag": member(0, 1)})

    w1_loads, w2_loads = [], []
    for k in (0, 3, 1, 2):
        for lane in (0, 1):
            for m in range(2):
                w1_loads.append(pltpu.make_async_copy(
                    modw.at[m, member(k, lane)],
                    w1.at[:, k * 2 + lane, :, pl.ds(m * part, part)], sem_w1.at[len(w1_loads)]))
            for m in range(3):
                w2_loads.append(pltpu.make_async_copy(
                    qkvw.at[m, member(k, lane)],
                    w2.at[:, k * 2 + lane, :, pl.ds(m * part, part)], sem_w2.at[len(w2_loads)]))
    own_loads = [
        pltpu.make_async_copy(tokens.at[:, pl.ds(c * LANES, LANES)],
                              buf1.at[c, 0, :, pl.ds(0, LANES)], sem_own.at[c])
        for c in range(chunks)
    ]
    for load in own_loads + w1_loads:
        load.start()

    barrier = pltpu.get_barrier_semaphore()
    for turn in range(1, homes):
        pl.semaphore_signal(barrier, inc=1, device_id={"dp": home(turn, 1)}, device_id_type=MESH)
    for step in range(1, 8):
        pl.semaphore_signal(barrier, inc=1, device_id={"bag": lax.rem(bag + step, 8)}, device_id_type=MESH)
    pl.semaphore_wait(barrier, homes - 1 + 7)

    def spread(rows, hot):
        def one(turn):
            hots[pl.ds(0, rows), pl.ds(pl.multiple_of(turn * cap, cap), cap)] = hot(turn)

        loop(0, homes, one)

    def bag_hot(turn):
        ids = lax.broadcasted_iota(jnp.int32, (pack, cap), 0)
        return (ids == table[pl.ds(home(turn, -1), 1), :]).astype(bf16)

    def home_hot(turn):
        ids = lax.broadcasted_iota(jnp.int32, (resident, cap), 1) + home(turn, -1) * cap
        return (ids == cols[pl.ds(0, resident), 1:2]).astype(bf16)

    half1 = resident // 2

    def project(c, k):
        def tile(index):
            lanes = pl.ds(pl.multiple_of(index * 256, 256), 256)
            weight = w1[c, pl.ds(2 * k, 2), :, lanes].reshape(2 * LANES, 256)
            value = jnp.dot(buf1[c, k], weight, preferred_element_type=f32)
            if c == 0 and k == 0:
                acc1[:, lanes] = value
            else:
                acc1[:, lanes] += value

        loop(0, 2 * part // 256, tile)

    rings = [
        Ring(lambda half, c=c: tokens.at[pl.ds(half * half1, half1), pl.ds(c * LANES, LANES)],
             buf1.at[c], s1.at[c], r1.at[c], places, lambda k, c=c: project(c, k))
        for c in range(chunks)
    ]
    for ring in rings:
        ring.start()
    for load in own_loads + w1_loads:
        load.wait()
    for load in w2_loads:
        load.start()
    rings[0].own()
    rings[0].relay()
    rings[1].own()
    rings[1].relay()
    rings[0].beside()
    rings[2].own()
    rings[2].relay()
    rings[1].beside()
    rings[2].beside()
    spread(pack, bag_hot)
    for ring in rings:
        ring.across()
    is_first = cols[pl.ds(0, resident), 2:3] == 0
    proj[...] = jnp.where(is_first, acc1[:, :part], acc1[:, part:]).astype(bf16)

    def to_bag(c, turn):
        return remote(sbuf.at[c, turn], abuf.at[c, turn], sa.at[c, turn], ra.at[c, turn], {"dp": home(turn, 1)})

    def to_home(c, turn):
        return remote(sbuf.at[c, turn], back.at[c, turn], sb.at[c, turn], rb.at[c, turn], {"dp": home(turn, 1)})

    def stay(c, target, sem):
        return pltpu.make_async_copy(sbuf.at[c, 0], target.at[c, 0], sem.at[c, 0])

    group = 4

    def launch(c, index, copy, target, sem):
        for j in range(group):
            if j == 0:
                @pl.when(index == 0)
                def _():
                    stay(c, target, sem).start()

                @pl.when(index > 0)
                def _():
                    copy(c, index * group).start()
            else:
                copy(c, index * group + j).start()

    def fill(first, last):
        def some(index):
            hots = []
            for j in range(group):
                ids = lax.broadcasted_iota(jnp.int32, (cap, resident), 0) + home(index * group + j, 1) * cap
                hots.append((own_row[...] == ids).astype(bf16))
            block = jnp.dot(jnp.concatenate(hots, axis=0), proj[:, first * LANES:last * LANES],
                            preferred_element_type=f32).astype(bf16)
            for c in range(first, last):
                for j in range(group):
                    sbuf[c, index * group + j] = block[j * cap:(j + 1) * cap, (c - first) * LANES:(c - first + 1) * LANES]
                launch(c, index, to_bag, abuf, ra)

        loop(0, homes // group, some)

    fill(0, 1)
    fill(1, chunks)
    for ring in rings:
        ring.finish()

    def collect(c, source, sem, copy, rows):
        acc_pick[pl.ds(0, rows), :] = jnp.zeros((rows, LANES), f32)

        def take(index):
            values = []
            for j in range(group):
                turn = index * group + j
                if j == 0:
                    @pl.when(index == 0)
                    def _():
                        stay(c, source, sem).wait()

                    @pl.when(index > 0)
                    def _():
                        copy(c, turn).wait_recv()
                else:
                    copy(c, turn).wait_recv()
                values.append(source[c, turn])
            span = pl.ds(pl.multiple_of(index * group * cap, group * cap), group * cap)
            acc_pick[pl.ds(0, rows), :] += jnp.dot(
                hots[pl.ds(0, rows), span], jnp.concatenate(values, axis=0), preferred_element_type=f32)

        loop(0, homes // group, take)
        return acc_pick[pl.ds(0, rows), :].astype(bf16)

    half2 = pack // 2

    def qkv(c, k):
        def tile(index):
            rows = pl.ds(pl.multiple_of(index * half2, half2), half2)
            weight = w2[c, pl.ds(2 * k, 2)].reshape(2 * LANES, 3 * part)
            value = jnp.dot(buf2[c, k, rows, :], weight, preferred_element_type=f32)
            if c == 0 and k == 0:
                acc2[rows, :] = value
            else:
                acc2[rows, :] += value

        loop(0, 2, tile)

    rings = [
        Ring(lambda half, c=c: buf2.at[c, 0, pl.ds(half * half2, half2), pl.ds(0, LANES)],
             buf2.at[c], s2.at[c], r2.at[c], places, lambda k, c=c: qkv(c, k))
        for c in range(chunks)
    ]

    def pack_in(c):
        buf2[c, 0, :, 0:LANES] = collect(c, abuf, ra, to_bag, pack)
        rings[c].start()

    pack_in(0)
    pack_in(1)
    rings[0].relay()
    for load in w2_loads:
        load.wait()
    rings[0].own()
    pack_in(2)
    rings[1].own()
    rings[1].relay()
    rings[0].beside()
    rings[2].own()
    spread(resident, home_hot)
    rings[0].across()
    rings[2].relay()

    def columns(index):
        return outw.at[:, :, pl.ds(pl.multiple_of(index * part, part), part)]

    w3_own = pltpu.make_async_copy(columns(bag), w3.at[:, 0], sem_own.at[chunks])
    w3_own.start()
    w3_copies = []
    for k in range(4):
        for lane in range(2):
            if k or lane:
                target = lax.rem(z + 4 - k, 4) * 2 + (core if lane == 0 else 1 - core)
                index = k * 2 + lane
                copy = remote(columns(target), w3.at[:, index], sem_w3s.at[index], sem_w3r.at[index],
                              {"bag": target})
                copy.start()
                w3_copies.append(copy)

    rings[1].beside()
    rings[1].across()
    rings[2].beside()
    rings[2].across()
    for c in range(chunks):
        stay_turns = lambda turn, c=c: to_bag(c, turn).wait_send()
        loop(1, homes, stay_turns)
    for ring in rings:
        ring.finish()

    block_rows = pack // 5

    def prepare(pair):
        key = head_scale(acc2[:, pl.ds(part + pair * LANES, LANES)], gain[1:2, pl.ds(pair * LANES, LANES)])
        value = acc2[:, pl.ds(2 * part + pair * LANES, LANES)].astype(bf16)
        low = lax.broadcasted_iota(jnp.int32, value.shape, 1) < HD
        for head in range(2):
            kx[head] = extend(key, cols[pl.ds(0, pack), 3:4], head == 0)
            vx[head] = jnp.where(low == (head == 0), value, jnp.ones_like(value))

    def attend(pair, index):
        lanes = pl.ds(pair * LANES, LANES)
        rows = pl.ds(pl.multiple_of(index * block_rows, block_rows), block_rows)
        query = head_scale(acc2[rows, lanes], gain[0:1, lanes])
        results = []
        for head in range(2):
            qx = extend(query, cols[rows, 3:4], head == 0)
            s = lax.dot_general(qx, kx[head], (((1,), (1,)), ((), ())), preferred_element_type=f32)
            top = jnp.max(s, axis=1, keepdims=True)
            p = jnp.exp2((s - top) * (LOG2E * HD ** -0.5)).astype(bf16)
            o = jnp.dot(p, vx[head], preferred_element_type=f32)
            results.append(o / pltpu.roll(o, HD, 1))
        low_out = lax.broadcasted_iota(jnp.int32, results[0].shape, 1) < HD
        att[rows, :] = jnp.where(low_out, results[0], results[1]).astype(bf16)

    def send_back(c):
        def some(index):
            hots = []
            for j in range(group):
                ids = lax.broadcasted_iota(jnp.int32, (cap, pack), 1)
                begin = pl.multiple_of(home(index * group + j, 1) * cap, cap)
                hots.append((cols[pl.ds(begin, cap), 0:1] == ids).astype(bf16))
            block = jnp.dot(jnp.concatenate(hots, axis=0), att[...], preferred_element_type=f32).astype(bf16)
            for j in range(group):
                sbuf[c, index * group + j] = block[j * cap:(j + 1) * cap]
            launch(c, index, to_home, back, rb)

        loop(0, homes // group, some)

    def finish(c, k):
        weight = w3[c, pl.ds(2 * k, 2)].reshape(2 * LANES, part)
        value = jnp.dot(buf3[c, k], weight, preferred_element_type=f32)
        if c == 0 and k == 0:
            acc3[...] = value
        elif c == chunks - 1 and k == 2:
            out[...] = (acc3[...] + value).astype(bf16)
        else:
            acc3[...] += value

    rings = [
        Ring(lambda half, c=c: buf3.at[c, 0, pl.ds(half * half1, half1), pl.ds(0, LANES)],
             buf3.at[c], s3.at[c], r3.at[c], places, lambda k, c=c: finish(c, k))
        for c in range(chunks)
    ]

    def home_in(c):
        buf3[c, 0, :, 0:LANES] = collect(c, back, rb, to_home, resident)
        rings[c].start()

    prepare(0)
    loop(0, 5, lambda index: attend(0, index))
    send_back(0)
    prepare(1)
    loop(0, 5, lambda index: attend(1, index))
    send_back(1)
    home_in(0)
    prepare(2)
    loop(0, 3, lambda index: attend(2, index))
    rings[0].relay()
    home_in(1)
    loop(3, 5, lambda index: attend(2, index))
    send_back(2)
    w3_own.wait()
    for copy in w3_copies:
        copy.wait()
    rings[1].relay()
    rings[0].own()
    rings[0].beside()
    rings[1].own()
    rings[0].across()
    home_in(2)
    rings[1].beside()
    rings[1].across()
    rings[2].own()
    rings[2].relay()
    rings[2].beside()
    rings[2].across()
    for c in range(chunks):
        loop(1, homes, lambda turn, c=c: to_home(c, turn).wait_send())
    for ring in rings:
        ring.finish()


def body(
    home_tokens,
    mod_weight,
    qkv_weight,
    norm_gain,
    output_weight,
    row_plan,
    sample_lengths,
    modality,
):
    homes = lax.axis_size("dp")
    my_home = lax.axis_index("dp")
    resident, part = home_tokens.shape
    full = mod_weight.shape[1]
    pack = resident + resident // 4
    cap = 2 * resident // homes
    slots = cap * homes
    own_index, slot_table, row_modality, sample_ids = plan_tables(
        row_plan, sample_lengths, modality, my_home, homes, resident, pack
    )

    def pad(values):
        return jnp.pad(values, (0, slots - values.shape[0]))

    cols = jnp.stack([slot_table, pad(own_index), pad(row_modality), pad(sample_ids)], axis=1)
    bf16, f32 = jnp.bfloat16, jnp.float32
    any_spec = pl.BlockSpec(memory_space=pl.ANY)
    vmem = pl.BlockSpec(memory_space=pltpu.VMEM)
    dma = pltpu.SemaphoreType.DMA
    chunks = part // LANES
    members = full // part
    kernel = functools.partial(mega_kernel, 4, 4)
    ring_sems = [dma((chunks, 14)), dma((chunks, 4, 2, 2))]
    return pl.pallas_call(
        kernel,
        out_shape=jax.ShapeDtypeStruct((resident, part), bf16),
        in_specs=[any_spec] * 4 + [vmem] * 4,
        out_specs=vmem,
        scratch_shapes=[
            pltpu.VMEM((chunks, 4, resident, 2 * LANES), bf16),
            pltpu.VMEM((chunks, members, LANES, 2 * part), bf16),
            pltpu.VMEM((resident, 2 * part), f32),
            pltpu.VMEM((resident, part), bf16),
            pltpu.VMEM((chunks, homes, cap, LANES), bf16),
            pltpu.VMEM((chunks, homes, cap, LANES), bf16),
            pltpu.VMEM((chunks, 4, pack, 2 * LANES), bf16),
            pltpu.VMEM((chunks, members, LANES, 3 * part), bf16),
            pltpu.VMEM((pack, 3 * part), f32),
            pltpu.VMEM((pack, LANES), f32),
            pltpu.VMEM((pack, slots), bf16),
            pltpu.VMEM((2, pack, LANES), bf16),
            pltpu.VMEM((2, pack, LANES), bf16),
            pltpu.VMEM((pack, LANES), bf16),
            pltpu.VMEM((chunks, homes, cap, LANES), bf16),
            pltpu.VMEM((chunks, 4, resident, 2 * LANES), bf16),
            pltpu.VMEM((chunks, members, LANES, part), bf16),
            pltpu.VMEM((resident, part), f32),
            dma((16,)), dma((24,)), dma((8,)), dma((8,)), dma((chunks + 1,)),
            *ring_sems, *ring_sems, *ring_sems,
            *[dma((chunks, homes))] * 4,
        ],
        compiler_params=pltpu.CompilerParams(
            collective_id=0, has_side_effects=True, vmem_limit_bytes=67043328),
        name="mega",
    )(
        home_tokens,
        mod_weight.reshape(2, members, chunks, LANES, part),
        qkv_weight.reshape(3, members, chunks, LANES, part),
        output_weight.reshape(chunks, LANES, full),
        norm_gain, own_index[None, :], slot_table.reshape(homes, cap), cols,
    )


def solution(mesh):
    in_specs = (
        P("dp", "bag"),
        P(None, None, "bag"),
        P(None, None, "bag"),
        P(None, "bag"),
        P("bag", None),
        P(),
        P(),
        P(),
    )
    return jax.shard_map(body, mesh=mesh, in_specs=in_specs, out_specs=P("dp", "bag"), check_vma=False)
```

```python
import functools

import jax
import jax.numpy as jnp
from jax import lax
from jax.experimental import pallas as pl
from jax.experimental.pallas import tpu as pltpu
from jax.sharding import PartitionSpec as P

HD = 64
EPS = 1e-06
LOG2E = 1.4426950408889634


def plan_tables(row_plan, sample_lengths, modality, my_home, homes, resident, pack):
    cap = 2 * resident // homes
    dest = row_plan.reshape(homes, resident)
    bag = dest // pack
    slot = dest % pack
    bag_ids = jnp.arange(homes, dtype=jnp.int32)
    onehot = (bag[:, :, None] == bag_ids).astype(jnp.bfloat16)
    row_ids = jnp.arange(resident, dtype=jnp.int32)
    lower = (row_ids[:, None] > row_ids[None, :]).astype(jnp.bfloat16)
    ahead = jnp.einsum("mt,pta->pma", lower, onehot, preferred_element_type=jnp.float32)
    position = jnp.sum(ahead * onehot.astype(jnp.float32), axis=2).astype(jnp.int32)
    key = jnp.where(bag == my_home, position, -1)
    cap_ids = jnp.arange(cap, dtype=jnp.int32)
    slot_table = jnp.sum(
        jnp.where(key[:, None, :] == cap_ids[None, :, None], slot[:, None, :] + 1, 0), axis=2
    ).reshape(homes * cap) - 1
    own_bag = lax.dynamic_index_in_dim(bag, my_home, 0, keepdims=False)
    own_slot = lax.dynamic_index_in_dim(slot, my_home, 0, keepdims=False)
    own_index = own_bag * cap + lax.dynamic_index_in_dim(position, my_home, 0, keepdims=False)
    ends = jnp.cumsum(sample_lengths, axis=1)
    hits = (own_bag[:, None] == bag_ids[None, :])[:, :, None]
    row_ends = jnp.sum(jnp.where(hits, ends[None], 0), axis=1)
    row_mods = jnp.sum(jnp.where(hits, modality[None], 0), axis=1)
    row_sample = jnp.sum((own_slot[:, None] >= row_ends).astype(jnp.int32), axis=1)
    pick = row_sample[:, None] == jnp.arange(ends.shape[1], dtype=jnp.int32)[None, :]
    row_modality = jnp.sum(jnp.where(pick, row_mods, 0), axis=1)
    my_ends = jnp.sum(jnp.where((bag_ids == my_home)[:, None], ends, 0), axis=0)
    slot_ids = jnp.arange(pack, dtype=jnp.int32)
    sample_ids = jnp.sum((slot_ids[:, None] >= my_ends[None, :]).astype(jnp.int32), axis=1)
    return own_index, slot_table, row_modality, sample_ids


MESH = pl.DeviceIdType.MESH
LANES = 128


def remote(src, dst, send_sem, recv_sem, where):
    return pltpu.make_async_remote_copy(
        src_ref=src, dst_ref=dst, send_sem=send_sem, recv_sem=recv_sem, device_id=where, device_id_type=MESH
    )


class Ring:
    def __init__(self, first, buf, send_sems, recv_sems, places, on_ready):
        self.first, self.buf, self.send_sems, self.recv_sems = first, buf, send_sems, recv_sems
        self.near, self.far, self.twin = places
        self.on_ready = on_ready
        self.half = buf.shape[1] // 2
        self.sent, self.lands = [], {}

    def rows(self, half):
        return pl.ds(half * self.half, self.half)

    def view(self, k, lane, half):
        return self.buf.at[k, self.rows(half), pl.ds(lane * LANES, LANES)]

    def send(self, source, half, k, lane, where):
        copy = remote(source, self.view(k, lane, half), self.send_sems.at[len(self.sent)],
                      self.recv_sems.at[k, lane, half], where)
        copy.start()
        self.sent.append(copy)
        self.lands[k, lane, half] = copy

    def start(self):
        self.send(self.first(0), 0, 3, 0, self.near)
        self.send(self.first(1), 1, 1, 0, self.far)
        self.send(self.first(0), 0, 0, 1, self.twin)
        self.send(self.first(1), 1, 0, 1, self.twin)
        self.send(self.first(1), 1, 3, 0, self.near)
        self.send(self.first(0), 0, 1, 0, self.far)

    def forward(self, k, half):
        self.lands[k, 0, half].wait_recv()
        self.send(self.view(k, 0, half), half, k, 1, self.twin)

    def ready(self, k):
        for half in (0, 1):
            self.lands[k, 1, half].wait_recv()
        self.on_ready(k)

    def relay(self):
        for k, half, where in ((3, 0, self.near), (1, 1, self.far)):
            self.lands[k, 0, half].wait_recv()
            self.send(self.view(k, 0, half), half, 2, 0, where)
            self.send(self.view(k, 0, half), half, k, 1, self.twin)

    def own(self):
        self.ready(0)

    def beside(self):
        self.forward(3, 1)
        self.forward(1, 0)
        self.ready(3)
        self.ready(1)

    def across(self):
        self.forward(2, 0)
        self.forward(2, 1)

    def last(self):
        self.ready(2)

    def finish(self):
        for copy in self.sent:
            copy.wait_send()


def loop(begin, end, step):
    def run(index, carry):
        step(index)
        return carry

    lax.fori_loop(begin, end, run, 0)


def head_scale(x, gain):
    low = lax.broadcasted_iota(jnp.int32, x.shape, 1) < HD

    def mean(t):
        left = jnp.sum(jnp.where(low, t, 0.0), axis=1, keepdims=True)
        right = jnp.sum(jnp.where(low, 0.0, t), axis=1, keepdims=True)
        return jnp.where(low, left, right) * (1.0 / HD)

    shifted = x - mean(x)
    return (shifted * lax.rsqrt(mean(shifted * shifted) + EPS) * gain).astype(jnp.bfloat16)


def extend(x, sample, keep_low):
    lane = lax.broadcasted_iota(jnp.int32, x.shape, 1)
    mark = jnp.where((lane % HD) == sample, 128.0, 0.0).astype(x.dtype)
    return jnp.where((lane < HD) == keep_low, x, mark)


def mega_kernel(
    homes_x, homes_y,
    tokens, modw, qkvw, outw, gain, own_row, table, cols,
    out,
    buf1, w1, acc1, proj, sbuf, abuf, buf2, w2, acc2, acc_pick, hots, qx, kx, vx, ahead, att, back, buf3, w3, acc3,
    sem_w1, sem_w2, sem_w3s, sem_w3r, sem_own,
    s1, r1, s2, r2, s3, r3, sa, ra, sb, rb,
):
    homes = homes_x * homes_y
    me = lax.axis_index("dp")
    bag = lax.axis_index("bag")
    x, y = lax.div(me, homes_y), lax.rem(me, homes_y)
    z, core = lax.div(bag, 2), lax.rem(bag, 2)
    resident, part = tokens.shape
    pack = buf2.shape[2]
    cap = sbuf.shape[2]
    chunks = part // LANES
    f32, bf16 = jnp.float32, jnp.bfloat16

    def member(k, lane):
        return lax.rem(z + k, 4) * 2 + (core if lane == 0 else 1 - core)

    def home(turn, sign):
        step = lax.rem(turn * 5, homes)
        dx, dy = lax.div(step, homes_y), lax.rem(step, homes_y)
        if sign < 0:
            dx, dy = homes_x - dx, homes_y - dy
        return lax.rem(x + dx, homes_x) * homes_y + lax.rem(y + dy, homes_y)

    places = ({"bag": member(1, 0)}, {"bag": member(3, 0)}, {"bag": member(0, 1)})

    w1_loads, w2_loads = [], []
    for k in (0, 3, 1, 2):
        for lane in (0, 1):
            for m in range(2):
                w1_loads.append(pltpu.make_async_copy(
                    modw.at[m, member(k, lane)],
                    w1.at[:, k * 2 + lane, :, pl.ds(m * part, part)], sem_w1.at[len(w1_loads)]))
            for m in range(3):
                w2_loads.append(pltpu.make_async_copy(
                    qkvw.at[m, member(k, lane)],
                    w2.at[:, k * 2 + lane, :, pl.ds(m * part, part)], sem_w2.at[len(w2_loads)]))
    own_loads = [
        pltpu.make_async_copy(tokens.at[:, pl.ds(c * LANES, LANES)],
                              buf1.at[c, 0, :, pl.ds(0, LANES)], sem_own.at[c])
        for c in range(chunks)
    ]
    for load in own_loads + w1_loads:
        load.start()

    barrier = pltpu.get_barrier_semaphore()
    for turn in range(1, homes):
        pl.semaphore_signal(barrier, inc=1, device_id={"dp": home(turn, 1)}, device_id_type=MESH)
    for step in range(1, 8):
        pl.semaphore_signal(barrier, inc=1, device_id={"bag": lax.rem(bag + step, 8)}, device_id_type=MESH)
    pl.semaphore_wait(barrier, homes - 1 + 7)

    def bag_block(index):
        return hots.at[index]

    def home_block(index):
        return buf1.at[lax.div(index, 4), lax.rem(index, 4)]

    def spread(block, hot):
        def one(index):
            block(index)[...] = jnp.concatenate([hot(2 * index), hot(2 * index + 1)], axis=1)

        loop(0, homes // 2, one)

    def bag_hot(turn):
        ids = lax.broadcasted_iota(jnp.int32, (pack, cap), 0)
        return (ids == table[pl.ds(home(turn, -1), 1), :]).astype(bf16)

    def home_hot(turn):
        ids = lax.broadcasted_iota(jnp.int32, (resident, cap), 1) + home(turn, -1) * cap
        return (ids == cols[pl.ds(0, resident), 1:2]).astype(bf16)

    half1 = resident // 2

    def project(c, k):
        def tile(index):
            lanes = pl.ds(pl.multiple_of(index * 256, 256), 256)
            weight = w1[c, pl.ds(2 * k, 2), :, lanes].reshape(2 * LANES, 256)
            value = jnp.dot(buf1[c, k], weight, preferred_element_type=f32)
            if c == 0 and k == 0:
                acc1[:, lanes] = value
            else:
                acc1[:, lanes] += value

        loop(0, 2 * part // 256, tile)

    rings = [
        Ring(lambda half, c=c: tokens.at[pl.ds(half * half1, half1), pl.ds(c * LANES, LANES)],
             buf1.at[c], s1.at[c], r1.at[c], places, lambda k, c=c: project(c, k))
        for c in range(chunks)
    ]
    for ring in rings:
        ring.start()
    for load in own_loads + w1_loads:
        load.wait()
    for load in w2_loads:
        load.start()
    rings[0].own()
    spread(bag_block, bag_hot)
    rings[0].relay()
    rings[1].own()
    rings[1].relay()
    rings[0].beside()
    rings[2].own()
    rings[2].relay()
    rings[1].beside()
    rings[0].across()
    rings[2].beside()
    rings[1].across()
    rings[0].last()
    rings[1].last()
    rings[2].across()
    rings[2].last()
    is_first = cols[pl.ds(0, resident), 2:3] == 0
    proj[...] = jnp.where(is_first, acc1[:, :part], acc1[:, part:]).astype(bf16)

    def to_bag(c, turn):
        return remote(sbuf.at[c, turn], abuf.at[c, turn], sa.at[c, turn], ra.at[c, turn], {"dp": home(turn, 1)})

    def to_home(c, turn):
        return remote(sbuf.at[c, turn], back.at[c, turn], sb.at[c, turn], rb.at[c, turn], {"dp": home(turn, 1)})

    def stay(c, target, sem):
        return pltpu.make_async_copy(sbuf.at[c, 0], target.at[c, 0], sem.at[c, 0])

    group = 4

    def launch(c, index, copy, target, sem):
        for j in range(group):
            if j == 0:
                @pl.when(index == 0)
                def _():
                    stay(c, target, sem).start()

                @pl.when(index > 0)
                def _():
                    copy(c, index * group).start()
            else:
                copy(c, index * group + j).start()

    def fill(first, last):
        def some(index):
            hots = []
            for j in range(group):
                ids = lax.broadcasted_iota(jnp.int32, (cap, resident), 0) + home(index * group + j, 1) * cap
                hots.append((own_row[...] == ids).astype(bf16))
            block = jnp.dot(jnp.concatenate(hots, axis=0), proj[:, first * LANES:last * LANES],
                            preferred_element_type=f32).astype(bf16)
            for c in range(first, last):
                for j in range(group):
                    sbuf[c, index * group + j] = block[j * cap:(j + 1) * cap, (c - first) * LANES:(c - first + 1) * LANES]
                if c == first:
                    launch(c, index, to_bag, abuf, ra)

        loop(0, homes // group, some)

    def columns(index):
        return outw.at[:, :, pl.ds(pl.multiple_of(index * part, part), part)]

    w3_own = pltpu.make_async_copy(columns(bag), w3.at[:, 0], sem_own.at[chunks])
    w3_copies = []

    def share(k):
        for lane in range(2):
            if k or lane:
                target = lax.rem(z + 4 - k, 4) * 2 + (core if lane == 0 else 1 - core)
                index = k * 2 + lane
                copy = remote(columns(target), w3.at[:, index], sem_w3s.at[index], sem_w3r.at[index],
                              {"bag": target})
                copy.start()
                w3_copies.append(copy)

    fill(0, 1)
    for k in (1, 3, 0):
        share(k)
    fill(1, chunks)
    for c in range(2, chunks):
        loop(0, homes // group, lambda index, c=c: launch(c, index, to_bag, abuf, ra))
    for ring in rings:
        ring.finish()

    def collect(c, source, sem, copy, rows, block):
        acc_pick[pl.ds(0, rows), :] = jnp.zeros((rows, LANES), f32)

        def take(index):
            values = []
            for j in range(group):
                turn = index * group + j
                if j == 0:
                    @pl.when(index == 0)
                    def _():
                        stay(c, source, sem).wait()

                    @pl.when(index > 0)
                    def _():
                        copy(c, turn).wait_recv()
                else:
                    copy(c, turn).wait_recv()
                values.append(source[c, turn])
            hot = jnp.concatenate([block(2 * index)[...], block(2 * index + 1)[...]], axis=1)
            acc_pick[pl.ds(0, rows), :] += jnp.dot(
                hot, jnp.concatenate(values, axis=0), preferred_element_type=f32)

        loop(0, homes // group, take)
        return acc_pick[pl.ds(0, rows), :].astype(bf16)

    half2 = pack // 2

    def qkv(c, k):
        def tile(index):
            rows = pl.ds(pl.multiple_of(index * half2, half2), half2)
            weight = w2[c, pl.ds(2 * k, 2)].reshape(2 * LANES, 3 * part)
            value = jnp.dot(buf2[c, k, rows, :], weight, preferred_element_type=f32)
            if c == 0 and k == 0:
                acc2[rows, :] = value
            else:
                acc2[rows, :] += value

        loop(0, 2, tile)

    rings = [
        Ring(lambda half, c=c: buf2.at[c, 0, pl.ds(half * half2, half2), pl.ds(0, LANES)],
             buf2.at[c], s2.at[c], r2.at[c], places, lambda k, c=c: qkv(c, k))
        for c in range(chunks)
    ]

    def pack_in(c):
        buf2[c, 0, :, 0:LANES] = collect(c, abuf, ra, to_bag, pack, bag_block)
        rings[c].start()

    pack_in(0)
    spread(home_block, home_hot)
    pack_in(1)
    rings[0].relay()
    for load in w2_loads:
        load.wait()
    rings[0].own()
    pack_in(2)
    rings[1].relay()
    rings[1].own()
    rings[0].beside()
    rings[2].own()
    rings[1].beside()
    rings[0].across()
    rings[2].relay()
    rings[0].last()
    rings[2].beside()
    rings[1].across()
    rings[1].last()
    rings[2].across()
    rings[2].last()
    for c in range(chunks):
        stay_turns = lambda turn, c=c: to_bag(c, turn).wait_send()
        loop(1, homes, stay_turns)
    for ring in rings:
        ring.finish()

    blocks = 5
    block_rows = pack // blocks

    def prepare(pair):
        key = head_scale(acc2[:, pl.ds(part + pair * LANES, LANES)], gain[1:2, pl.ds(pair * LANES, LANES)])
        value = acc2[:, pl.ds(2 * part + pair * LANES, LANES)].astype(bf16)
        low = lax.broadcasted_iota(jnp.int32, value.shape, 1) < HD
        query = head_scale(acc2[:, pl.ds(pair * LANES, LANES)], gain[0:1, pl.ds(pair * LANES, LANES)])
        for head in range(2):
            qx[head] = extend(query, cols[pl.ds(0, pack), 3:4], head == 0)
            kx[head] = extend(key, cols[pl.ds(0, pack), 3:4], head == 0)
            vx[head] = jnp.where(low == (head == 0), value, jnp.ones_like(value))
        ahead[...] = score(0, 0)

    def score(head, index):
        rows = pl.ds(pl.multiple_of(index * block_rows, block_rows), block_rows)
        return lax.dot_general(qx[head, rows, :], kx[head], (((1,), (1,)), ((), ())), preferred_element_type=f32)

    def weigh(head, s):
        top = jnp.max(s, axis=1, keepdims=True)
        p = jnp.exp2((s - top) * (LOG2E * HD ** -0.5)).astype(bf16)
        o = jnp.dot(p, vx[head], preferred_element_type=f32)
        return o / pltpu.roll(o, HD, 1)

    def attend(index):
        rows = pl.ds(pl.multiple_of(index * block_rows, block_rows), block_rows)
        odd_scores = score(1, index)
        even = weigh(0, ahead[...])
        ahead[...] = score(0, lax.rem(index + 1, blocks))
        odd = weigh(1, odd_scores)
        low = lax.broadcasted_iota(jnp.int32, even.shape, 1) < HD
        att[rows, :] = jnp.where(low, even, odd).astype(bf16)

    def send_back(c):
        def some(index):
            hots = []
            for j in range(group):
                ids = lax.broadcasted_iota(jnp.int32, (cap, pack), 1)
                begin = pl.multiple_of(home(index * group + j, 1) * cap, cap)
                hots.append((cols[pl.ds(begin, cap), 0:1] == ids).astype(bf16))
            block = jnp.dot(jnp.concatenate(hots, axis=0), att[...], preferred_element_type=f32).astype(bf16)
            for j in range(group):
                sbuf[c, index * group + j] = block[j * cap:(j + 1) * cap]
            launch(c, index, to_home, back, rb)

        loop(0, homes // group, some)

    def finish(c, k):
        weight = w3[c, pl.ds(2 * k, 2)].reshape(2 * LANES, part)
        value = jnp.dot(buf3[c, k], weight, preferred_element_type=f32)
        if c == 0 and k == 0:
            acc3[...] = value
        elif c == chunks - 1 and k == 2:
            out[...] = (acc3[...] + value).astype(bf16)
        else:
            acc3[...] += value

    rings = [
        Ring(lambda half, c=c: buf3.at[c, 0, pl.ds(half * half1, half1), pl.ds(0, LANES)],
             buf3.at[c], s3.at[c], r3.at[c], places, lambda k, c=c: finish(c, k))
        for c in range(chunks)
    ]

    def home_in(c):
        buf3[c, 0, :, 0:LANES] = collect(c, back, rb, to_home, resident, home_block)
        rings[c].start()

    prepare(0)
    loop(0, 1, attend)
    w3_own.start()
    share(2)
    loop(1, blocks, attend)
    send_back(0)
    prepare(1)
    loop(0, blocks, attend)
    send_back(1)
    home_in(0)
    prepare(2)
    loop(0, 3, attend)
    rings[0].relay()
    home_in(1)
    loop(3, blocks, attend)
    send_back(2)
    rings[1].relay()
    w3_own.wait()
    for copy in w3_copies:
        copy.wait()
    rings[0].own()
    rings[0].beside()
    rings[0].across()
    rings[1].own()
    rings[0].last()
    home_in(2)
    rings[1].beside()
    rings[1].across()
    rings[2].own()
    rings[1].last()
    rings[2].relay()
    rings[2].beside()
    rings[2].across()
    rings[2].last()
    for c in range(chunks):
        loop(1, homes, lambda turn, c=c: to_home(c, turn).wait_send())
    for ring in rings:
        ring.finish()


def body(
    home_tokens,
    mod_weight,
    qkv_weight,
    norm_gain,
    output_weight,
    row_plan,
    sample_lengths,
    modality,
):
    homes = lax.axis_size("dp")
    my_home = lax.axis_index("dp")
    resident, part = home_tokens.shape
    full = mod_weight.shape[1]
    pack = resident + resident // 4
    cap = 2 * resident // homes
    slots = cap * homes
    own_index, slot_table, row_modality, sample_ids = plan_tables(
        row_plan, sample_lengths, modality, my_home, homes, resident, pack
    )

    def pad(values):
        return jnp.pad(values, (0, slots - values.shape[0]))

    cols = jnp.stack([slot_table, pad(own_index), pad(row_modality), pad(sample_ids)], axis=1)
    bf16, f32 = jnp.bfloat16, jnp.float32
    any_spec = pl.BlockSpec(memory_space=pl.ANY)
    vmem = pl.BlockSpec(memory_space=pltpu.VMEM)
    dma = pltpu.SemaphoreType.DMA
    chunks = part // LANES
    members = full // part
    kernel = functools.partial(mega_kernel, 4, 4)
    ring_sems = [dma((chunks, 14)), dma((chunks, 4, 2, 2))]
    return pl.pallas_call(
        kernel,
        out_shape=jax.ShapeDtypeStruct((resident, part), bf16),
        in_specs=[any_spec] * 4 + [vmem] * 4,
        out_specs=vmem,
        scratch_shapes=[
            pltpu.VMEM((chunks, 4, resident, 2 * LANES), bf16),
            pltpu.VMEM((chunks, members, LANES, 2 * part), bf16),
            pltpu.VMEM((resident, 2 * part), f32),
            pltpu.VMEM((resident, part), bf16),
            pltpu.VMEM((chunks, homes, cap, LANES), bf16),
            pltpu.VMEM((chunks, homes, cap, LANES), bf16),
            pltpu.VMEM((chunks, 4, pack, 2 * LANES), bf16),
            pltpu.VMEM((chunks, members, LANES, 3 * part), bf16),
            pltpu.VMEM((pack, 3 * part), f32),
            pltpu.VMEM((pack, LANES), f32),
            pltpu.VMEM((homes // 2, pack, 2 * LANES), bf16),
            pltpu.VMEM((2, pack, LANES), bf16),
            pltpu.VMEM((2, pack, LANES), bf16),
            pltpu.VMEM((2, pack, LANES), bf16),
            pltpu.VMEM((pack // 5, pack), f32),
            pltpu.VMEM((pack, LANES), bf16),
            pltpu.VMEM((chunks, homes, cap, LANES), bf16),
            pltpu.VMEM((chunks, 4, resident, 2 * LANES), bf16),
            pltpu.VMEM((chunks, members, LANES, part), bf16),
            pltpu.VMEM((resident, part), f32),
            dma((16,)), dma((24,)), dma((8,)), dma((8,)), dma((chunks + 1,)),
            *ring_sems, *ring_sems, *ring_sems,
            *[dma((chunks, homes))] * 4,
        ],
        compiler_params=pltpu.CompilerParams(
            collective_id=0, has_side_effects=True, vmem_limit_bytes=67043328),
        name="mega",
    )(
        home_tokens,
        mod_weight.reshape(2, members, chunks, LANES, part),
        qkv_weight.reshape(3, members, chunks, LANES, part),
        output_weight.reshape(chunks, LANES, full),
        norm_gain, own_index[None, :], slot_table.reshape(homes, cap), cols,
    )


def solution(mesh):
    in_specs = (
        P("dp", "bag"),
        P(None, None, "bag"),
        P(None, None, "bag"),
        P(None, "bag"),
        P("bag", None),
        P(),
        P(),
        P(),
    )
    return jax.shard_map(body, mesh=mesh, in_specs=in_specs, out_specs=P("dp", "bag"), check_vma=False)
```

```python
import functools

import jax
import jax.numpy as jnp
from jax import lax
from jax.experimental import pallas as pl
from jax.experimental.pallas import tpu as pltpu
from jax.sharding import PartitionSpec as P

HD = 64
EPS = 1e-06
LOG2E = 1.4426950408889634


MESH = pl.DeviceIdType.MESH
LANES = 128


def remote(src, dst, send_sem, recv_sem, where):
    return pltpu.make_async_remote_copy(
        src_ref=src, dst_ref=dst, send_sem=send_sem, recv_sem=recv_sem, device_id=where, device_id_type=MESH
    )


class Ring:
    def __init__(self, first, buf, send_sems, recv_sems, places, on_ready):
        self.first, self.buf, self.send_sems, self.recv_sems = first, buf, send_sems, recv_sems
        self.near, self.far, self.twin = places
        self.on_ready = on_ready
        self.half = buf.shape[1] // 2
        self.sent, self.lands = [], {}

    def rows(self, half):
        return pl.ds(half * self.half, self.half)

    def view(self, k, lane, half):
        return self.buf.at[k, self.rows(half), pl.ds(lane * LANES, LANES)]

    def send(self, source, half, k, lane, where):
        copy = remote(source, self.view(k, lane, half), self.send_sems.at[len(self.sent)],
                      self.recv_sems.at[k, lane, half], where)
        copy.start()
        self.sent.append(copy)
        self.lands[k, lane, half] = copy

    def start(self):
        self.send(self.first(0), 0, 3, 0, self.near)
        self.send(self.first(1), 1, 1, 0, self.far)
        self.send(self.first(0), 0, 0, 1, self.twin)
        self.send(self.first(1), 1, 0, 1, self.twin)
        self.send(self.first(1), 1, 3, 0, self.near)
        self.send(self.first(0), 0, 1, 0, self.far)

    def forward(self, k, half):
        self.lands[k, 0, half].wait_recv()
        self.send(self.view(k, 0, half), half, k, 1, self.twin)

    def ready(self, k):
        for half in (0, 1):
            self.lands[k, 1, half].wait_recv()
        self.on_ready(k)

    def relay(self):
        for k, half, where in ((3, 0, self.near), (1, 1, self.far)):
            self.lands[k, 0, half].wait_recv()
            self.send(self.view(k, 0, half), half, 2, 0, where)
            self.send(self.view(k, 0, half), half, k, 1, self.twin)

    def own(self):
        self.ready(0)

    def beside(self):
        self.forward(3, 1)
        self.forward(1, 0)
        self.ready(3)
        self.ready(1)

    def across(self):
        self.forward(2, 0)
        self.forward(2, 1)

    def last(self):
        self.ready(2)

    def finish(self):
        for copy in self.sent:
            copy.wait_send()


def loop(begin, end, step):
    def run(index, carry):
        step(index)
        return carry

    lax.fori_loop(begin, end, run, 0)


def head_scale(x, gain):
    low = lax.broadcasted_iota(jnp.int32, x.shape, 1) < HD

    def mean(t):
        left = jnp.sum(jnp.where(low, t, 0.0), axis=1, keepdims=True)
        right = jnp.sum(jnp.where(low, 0.0, t), axis=1, keepdims=True)
        return jnp.where(low, left, right) * (1.0 / HD)

    shifted = x - mean(x)
    return (shifted * lax.rsqrt(mean(shifted * shifted) + EPS) * gain).astype(jnp.bfloat16)


def extend(x, sample, keep_low):
    lane = lax.broadcasted_iota(jnp.int32, x.shape, 1)
    mark = jnp.where((lane % HD) == sample, 128.0, 0.0).astype(x.dtype)
    return jnp.where((lane < HD) == keep_low, x, mark)


def mega_kernel(
    homes_x, homes_y,
    tokens, modw, qkvw, outw, gain, plan, lengths, modality,
    out,
    own_row, table, cols, keys, buf1, w1, acc1, proj, sbuf, abuf, buf2, w2, acc2, acc_pick, hots, qx, kx, vx, ahead, att, back, buf3, w3, acc3,
    sem_w1, sem_w2, sem_w3s, sem_w3r, sem_own,
    s1, r1, s2, r2, s3, r3, sa, ra, sb, rb,
):
    homes = homes_x * homes_y
    me = lax.axis_index("dp")
    bag = lax.axis_index("bag")
    x, y = lax.div(me, homes_y), lax.rem(me, homes_y)
    z, core = lax.div(bag, 2), lax.rem(bag, 2)
    resident, part = tokens.shape
    pack = buf2.shape[2]
    cap = sbuf.shape[2]
    chunks = part // LANES
    f32, bf16 = jnp.float32, jnp.bfloat16

    def member(k, lane):
        return lax.rem(z + k, 4) * 2 + (core if lane == 0 else 1 - core)

    def home(turn, sign):
        step = lax.rem(turn * 5, homes)
        dx, dy = lax.div(step, homes_y), lax.rem(step, homes_y)
        if sign < 0:
            dx, dy = homes_x - dx, homes_y - dy
        return lax.rem(x + dx, homes_x) * homes_y + lax.rem(y + dy, homes_y)

    places = ({"bag": member(1, 0)}, {"bag": member(3, 0)}, {"bag": member(0, 1)})

    w1_loads, w2_loads = [], []
    for k in (0, 3, 1, 2):
        for lane in (0, 1):
            for m in range(2):
                w1_loads.append(pltpu.make_async_copy(
                    modw.at[m, member(k, lane)],
                    w1.at[:, k * 2 + lane, :, pl.ds(m * part, part)], sem_w1.at[len(w1_loads)]))
            for m in range(3):
                w2_loads.append(pltpu.make_async_copy(
                    qkvw.at[m, member(k, lane)],
                    w2.at[:, k * 2 + lane, :, pl.ds(m * part, part)], sem_w2.at[len(w2_loads)]))
    own_loads = [
        pltpu.make_async_copy(tokens.at[:, pl.ds(c * LANES, LANES)],
                              buf1.at[c, 0, :, pl.ds(0, LANES)], sem_own.at[c])
        for c in range(chunks)
    ]
    for load in own_loads + w1_loads:
        load.start()

    barrier = pltpu.get_barrier_semaphore()
    for turn in range(1, homes):
        pl.semaphore_signal(barrier, inc=1, device_id={"dp": home(turn, 1)}, device_id_type=MESH)
    for step in range(1, 8):
        pl.semaphore_signal(barrier, inc=1, device_id={"bag": lax.rem(bag + step, 8)}, device_id_type=MESH)
    pl.semaphore_wait(barrier, homes - 1 + 7)

    def bag_block(index):
        return hots.at[index]

    def home_block(index):
        return buf1.at[lax.div(index, 4), lax.rem(index, 4)]

    def spread(block, hot):
        def one(index):
            block(index)[...] = jnp.concatenate([hot(2 * index), hot(2 * index + 1)], axis=1)

        loop(0, homes // 2, one)

    def bag_hot(turn):
        ids = lax.broadcasted_iota(jnp.int32, (pack, cap), 0)
        return (ids == table[pl.ds(home(turn, -1), 1), :]).astype(bf16)

    def home_hot(turn):
        ids = lax.broadcasted_iota(jnp.int32, (resident, cap), 1) + home(turn, -1) * cap
        return (ids == cols[pl.ds(0, resident), 1:2]).astype(bf16)

    def split(rows):
        bags = ((rows.astype(f32) + 0.5) * (1.0 / pack)).astype(jnp.int32)
        return bags, rows - bags * pack

    def ends_of(index):
        ends = [lengths[index, 0]]
        for sample in range(1, lengths.shape[1]):
            ends.append(ends[-1] + lengths[index, sample])
        return ends

    def contract(left, right):
        return lax.dot_general(left, right, (((1,), (1,)), ((), ())), preferred_element_type=f32)

    def tables():
        for piece in range(resident // 256):
            before = lax.broadcasted_iota(jnp.int32, (resident, 256), 0)
            after = lax.broadcasted_iota(jnp.int32, (resident, 256), 1) + piece * 256
            hots[piece, 0:resident, :] = (before < after).astype(bf16)
        bags, _ = split(plan[...])
        own_bag, own_slot = split(plan[pl.ds(me, 1), :])
        mine = bags == me
        each = own_bag == lax.broadcasted_iota(jnp.int32, (homes, resident), 0)
        both = jnp.concatenate([mine.astype(bf16), each.astype(bf16)], axis=0)
        ranks = jnp.concatenate(
            [jnp.dot(both, hots[piece, 0:resident, :], preferred_element_type=f32)
             for piece in range(resident // 256)], axis=1)
        keys[...] = jnp.where(mine, ranks[:homes].astype(jnp.int32), -1)
        place = jnp.sum(jnp.where(each, ranks[homes:], 0.0), axis=0, keepdims=True).astype(jnp.int32)
        own_row[...] = own_bag * cap + place
        kind = jnp.zeros_like(own_bag)
        for index in range(homes):
            ends = ends_of(index)
            value = jnp.full_like(own_bag, 0) + modality[index, len(ends) - 1]
            for sample in range(len(ends) - 2, -1, -1):
                value = jnp.where(own_slot < ends[sample], modality[index, sample], value)
            kind = jnp.where(own_bag == index, value, kind)
        line = lax.broadcasted_iota(jnp.int32, (8, resident), 0)
        facts = jnp.where(line == 0, own_bag, jnp.where(line == 1, place, kind)).astype(bf16)

        def same(index):
            at = pl.multiple_of(index * 128, 128)
            own = lax.broadcasted_iota(jnp.int32, (128, resident), 0) + at
            hot = (own == lax.broadcasted_iota(jnp.int32, (128, resident), 1)).astype(bf16)
            got = contract(hot, facts).astype(jnp.int32)
            cols[pl.ds(at, 128), 1:2] = got[:, 0:1] * cap + got[:, 1:2]
            cols[pl.ds(at, 128), 2:3] = got[:, 2:3]

        loop(0, resident // 128, same)

        def slots_of(index):
            _, slot = split(plan[pl.ds(index, 1), :])
            high = lax.shift_right_logical(slot, 8)
            parts = jnp.where(line == 0, high, jnp.where(line == 1, slot - high * 256, 1)).astype(bf16)
            hot = (lax.broadcasted_iota(jnp.int32, (cap, resident), 0) == keys[pl.ds(index, 1), :]).astype(bf16)
            row = contract(parts, hot).astype(jnp.int32)
            table[pl.ds(index, 1), :] = jnp.where(row[2:3] > 0, row[0:1] * 256 + row[1:2], -1)
            col = contract(hot, parts).astype(jnp.int32)
            at = pl.multiple_of(index * cap, cap)
            cols[pl.ds(at, cap), 0:1] = jnp.where(col[:, 2:3] > 0, col[:, 0:1] * 256 + col[:, 1:2], -1)

        loop(0, homes, slots_of)
        here = lax.broadcasted_iota(jnp.int32, (pack, 1), 0)
        sample = jnp.zeros_like(here)
        for end in ends_of(me):
            sample = sample + (here >= end).astype(jnp.int32)
        cols[pl.ds(0, pack), 3:4] = sample

    half1 = resident // 2

    def project(c, k):
        def tile(index):
            lanes = pl.ds(pl.multiple_of(index * 256, 256), 256)
            weight = w1[c, pl.ds(2 * k, 2), :, lanes].reshape(2 * LANES, 256)
            value = jnp.dot(buf1[c, k], weight, preferred_element_type=f32)
            if c == 0 and k == 0:
                acc1[:, lanes] = value
            else:
                acc1[:, lanes] += value

        loop(0, 2 * part // 256, tile)

    rings = [
        Ring(lambda half, c=c: tokens.at[pl.ds(half * half1, half1), pl.ds(c * LANES, LANES)],
             buf1.at[c], s1.at[c], r1.at[c], places, lambda k, c=c: project(c, k))
        for c in range(chunks)
    ]
    for ring in rings:
        ring.start()
    tables()
    for load in own_loads + w1_loads:
        load.wait()
    for load in w2_loads:
        load.start()
    rings[0].own()
    spread(bag_block, bag_hot)
    rings[0].relay()
    rings[1].own()
    rings[1].relay()
    rings[0].beside()
    rings[2].own()
    rings[2].relay()
    rings[1].beside()
    rings[0].across()
    rings[2].beside()
    rings[1].across()
    rings[0].last()
    rings[1].last()
    rings[2].across()
    rings[2].last()
    is_first = cols[pl.ds(0, resident), 2:3] == 0
    proj[...] = jnp.where(is_first, acc1[:, :part], acc1[:, part:]).astype(bf16)

    def to_bag(c, turn):
        return remote(sbuf.at[c, turn], abuf.at[c, turn], sa.at[c, turn], ra.at[c, turn], {"dp": home(turn, 1)})

    def to_home(c, turn):
        return remote(sbuf.at[c, turn], back.at[c, turn], sb.at[c, turn], rb.at[c, turn], {"dp": home(turn, 1)})

    def stay(c, target, sem):
        return pltpu.make_async_copy(sbuf.at[c, 0], target.at[c, 0], sem.at[c, 0])

    group = 4

    def launch(c, index, copy, target, sem):
        for j in range(group):
            if j == 0:
                @pl.when(index == 0)
                def _():
                    stay(c, target, sem).start()

                @pl.when(index > 0)
                def _():
                    copy(c, index * group).start()
            else:
                copy(c, index * group + j).start()

    def fill(first, last):
        def some(index):
            hots = []
            for j in range(group):
                ids = lax.broadcasted_iota(jnp.int32, (cap, resident), 0) + home(index * group + j, 1) * cap
                hots.append((own_row[...] == ids).astype(bf16))
            block = jnp.dot(jnp.concatenate(hots, axis=0), proj[:, first * LANES:last * LANES],
                            preferred_element_type=f32).astype(bf16)
            for c in range(first, last):
                for j in range(group):
                    sbuf[c, index * group + j] = block[j * cap:(j + 1) * cap, (c - first) * LANES:(c - first + 1) * LANES]
                if c == first:
                    launch(c, index, to_bag, abuf, ra)

        loop(0, homes // group, some)

    def columns(index):
        return outw.at[:, :, pl.ds(pl.multiple_of(index * part, part), part)]

    w3_own = pltpu.make_async_copy(columns(bag), w3.at[:, 0], sem_own.at[chunks])
    w3_copies = []

    def share(k):
        for lane in range(2):
            if k or lane:
                target = lax.rem(z + 4 - k, 4) * 2 + (core if lane == 0 else 1 - core)
                index = k * 2 + lane
                copy = remote(columns(target), w3.at[:, index], sem_w3s.at[index], sem_w3r.at[index],
                              {"bag": target})
                copy.start()
                w3_copies.append(copy)

    fill(0, 1)
    for k in (1, 3, 0):
        share(k)
    fill(1, chunks)
    for c in range(2, chunks):
        loop(0, homes // group, lambda index, c=c: launch(c, index, to_bag, abuf, ra))
    for ring in rings:
        ring.finish()

    def collect(c, source, sem, copy, rows, block):
        acc_pick[pl.ds(0, rows), :] = jnp.zeros((rows, LANES), f32)

        def take(index):
            values = []
            for j in range(group):
                turn = index * group + j
                if j == 0:
                    @pl.when(index == 0)
                    def _():
                        stay(c, source, sem).wait()

                    @pl.when(index > 0)
                    def _():
                        copy(c, turn).wait_recv()
                else:
                    copy(c, turn).wait_recv()
                values.append(source[c, turn])
            hot = jnp.concatenate([block(2 * index)[...], block(2 * index + 1)[...]], axis=1)
            acc_pick[pl.ds(0, rows), :] += jnp.dot(
                hot, jnp.concatenate(values, axis=0), preferred_element_type=f32)

        loop(0, homes // group, take)
        return acc_pick[pl.ds(0, rows), :].astype(bf16)

    half2 = pack // 2

    def qkv(c, k):
        def tile(index):
            rows = pl.ds(pl.multiple_of(index * half2, half2), half2)
            weight = w2[c, pl.ds(2 * k, 2)].reshape(2 * LANES, 3 * part)
            value = jnp.dot(buf2[c, k, rows, :], weight, preferred_element_type=f32)
            if c == 0 and k == 0:
                acc2[rows, :] = value
            else:
                acc2[rows, :] += value

        loop(0, 2, tile)

    rings = [
        Ring(lambda half, c=c: buf2.at[c, 0, pl.ds(half * half2, half2), pl.ds(0, LANES)],
             buf2.at[c], s2.at[c], r2.at[c], places, lambda k, c=c: qkv(c, k))
        for c in range(chunks)
    ]

    def pack_in(c):
        buf2[c, 0, :, 0:LANES] = collect(c, abuf, ra, to_bag, pack, bag_block)
        rings[c].start()

    pack_in(0)
    spread(home_block, home_hot)
    pack_in(1)
    rings[0].relay()
    for load in w2_loads:
        load.wait()
    rings[0].own()
    pack_in(2)
    rings[1].relay()
    rings[1].own()
    rings[0].beside()
    rings[2].own()
    rings[1].beside()
    rings[0].across()
    rings[2].relay()
    rings[0].last()
    rings[2].beside()
    rings[1].across()
    rings[1].last()
    rings[2].across()
    rings[2].last()
    for c in range(chunks):
        stay_turns = lambda turn, c=c: to_bag(c, turn).wait_send()
        loop(1, homes, stay_turns)
    for ring in rings:
        ring.finish()

    blocks = 5
    block_rows = pack // blocks

    def prepare(pair):
        key = head_scale(acc2[:, pl.ds(part + pair * LANES, LANES)], gain[1:2, pl.ds(pair * LANES, LANES)])
        value = acc2[:, pl.ds(2 * part + pair * LANES, LANES)].astype(bf16)
        low = lax.broadcasted_iota(jnp.int32, value.shape, 1) < HD
        query = head_scale(acc2[:, pl.ds(pair * LANES, LANES)], gain[0:1, pl.ds(pair * LANES, LANES)])
        for head in range(2):
            qx[head] = extend(query, cols[pl.ds(0, pack), 3:4], head == 0)
            kx[head] = extend(key, cols[pl.ds(0, pack), 3:4], head == 0)
            vx[head] = jnp.where(low == (head == 0), value, jnp.ones_like(value))
        ahead[...] = score(0, 0)

    def score(head, index):
        rows = pl.ds(pl.multiple_of(index * block_rows, block_rows), block_rows)
        return lax.dot_general(qx[head, rows, :], kx[head], (((1,), (1,)), ((), ())), preferred_element_type=f32)

    def weigh(head, s):
        top = jnp.max(s, axis=1, keepdims=True)
        p = jnp.exp2((s - top) * (LOG2E * HD ** -0.5)).astype(bf16)
        o = jnp.dot(p, vx[head], preferred_element_type=f32)
        return o / pltpu.roll(o, HD, 1)

    def attend(index):
        rows = pl.ds(pl.multiple_of(index * block_rows, block_rows), block_rows)
        odd_scores = score(1, index)
        even = weigh(0, ahead[...])
        ahead[...] = score(0, lax.rem(index + 1, blocks))
        odd = weigh(1, odd_scores)
        low = lax.broadcasted_iota(jnp.int32, even.shape, 1) < HD
        att[rows, :] = jnp.where(low, even, odd).astype(bf16)

    def send_back(c):
        def some(index):
            hots = []
            for j in range(group):
                ids = lax.broadcasted_iota(jnp.int32, (cap, pack), 1)
                begin = pl.multiple_of(home(index * group + j, 1) * cap, cap)
                hots.append((cols[pl.ds(begin, cap), 0:1] == ids).astype(bf16))
            block = jnp.dot(jnp.concatenate(hots, axis=0), att[...], preferred_element_type=f32).astype(bf16)
            for j in range(group):
                sbuf[c, index * group + j] = block[j * cap:(j + 1) * cap]
            launch(c, index, to_home, back, rb)

        loop(0, homes // group, some)

    def finish(c, k):
        weight = w3[c, pl.ds(2 * k, 2)].reshape(2 * LANES, part)
        value = jnp.dot(buf3[c, k], weight, preferred_element_type=f32)
        if c == 0 and k == 0:
            acc3[...] = value
        elif c == chunks - 1 and k == 2:
            out[...] = (acc3[...] + value).astype(bf16)
        else:
            acc3[...] += value

    rings = [
        Ring(lambda half, c=c: buf3.at[c, 0, pl.ds(half * half1, half1), pl.ds(0, LANES)],
             buf3.at[c], s3.at[c], r3.at[c], places, lambda k, c=c: finish(c, k))
        for c in range(chunks)
    ]

    def home_in(c):
        buf3[c, 0, :, 0:LANES] = collect(c, back, rb, to_home, resident, home_block)
        rings[c].start()

    prepare(0)
    loop(0, 1, attend)
    w3_own.start()
    share(2)
    loop(1, blocks, attend)
    send_back(0)
    prepare(1)
    loop(0, blocks, attend)
    send_back(1)
    home_in(0)
    prepare(2)
    loop(0, 3, attend)
    rings[0].relay()
    home_in(1)
    loop(3, blocks, attend)
    send_back(2)
    rings[1].relay()
    w3_own.wait()
    for copy in w3_copies:
        copy.wait()
    rings[0].own()
    rings[0].beside()
    rings[0].across()
    rings[1].own()
    rings[0].last()
    home_in(2)
    rings[1].beside()
    rings[1].across()
    rings[2].own()
    rings[1].last()
    rings[2].relay()
    rings[2].beside()
    rings[2].across()
    rings[2].last()
    for c in range(chunks):
        loop(1, homes, lambda turn, c=c: to_home(c, turn).wait_send())
    for ring in rings:
        ring.finish()


def body(
    home_tokens,
    mod_weight,
    qkv_weight,
    norm_gain,
    output_weight,
    row_plan,
    sample_lengths,
    modality,
):
    homes = lax.axis_size("dp")
    resident, part = home_tokens.shape
    full = mod_weight.shape[1]
    pack = resident + resident // 4
    cap = 2 * resident // homes
    slots = cap * homes
    bf16, f32 = jnp.bfloat16, jnp.float32
    any_spec = pl.BlockSpec(memory_space=pl.ANY)
    vmem = pl.BlockSpec(memory_space=pltpu.VMEM)
    smem = pl.BlockSpec(memory_space=pltpu.SMEM)
    dma = pltpu.SemaphoreType.DMA
    chunks = part // LANES
    members = full // part
    kernel = functools.partial(mega_kernel, 4, 4)
    ring_sems = [dma((chunks, 14)), dma((chunks, 4, 2, 2))]
    return pl.pallas_call(
        kernel,
        out_shape=jax.ShapeDtypeStruct((resident, part), bf16),
        in_specs=[any_spec] * 4 + [vmem] * 2 + [smem] * 2,
        out_specs=vmem,
        scratch_shapes=[
            pltpu.VMEM((1, resident), jnp.int32),
            pltpu.VMEM((homes, cap), jnp.int32),
            pltpu.VMEM((slots, 4), jnp.int32),
            pltpu.VMEM((homes, resident), jnp.int32),
            pltpu.VMEM((chunks, 4, resident, 2 * LANES), bf16),
            pltpu.VMEM((chunks, members, LANES, 2 * part), bf16),
            pltpu.VMEM((resident, 2 * part), f32),
            pltpu.VMEM((resident, part), bf16),
            pltpu.VMEM((chunks, homes, cap, LANES), bf16),
            pltpu.VMEM((chunks, homes, cap, LANES), bf16),
            pltpu.VMEM((chunks, 4, pack, 2 * LANES), bf16),
            pltpu.VMEM((chunks, members, LANES, 3 * part), bf16),
            pltpu.VMEM((pack, 3 * part), f32),
            pltpu.VMEM((pack, LANES), f32),
            pltpu.VMEM((homes // 2, pack, 2 * LANES), bf16),
            pltpu.VMEM((2, pack, LANES), bf16),
            pltpu.VMEM((2, pack, LANES), bf16),
            pltpu.VMEM((2, pack, LANES), bf16),
            pltpu.VMEM((pack // 5, pack), f32),
            pltpu.VMEM((pack, LANES), bf16),
            pltpu.VMEM((chunks, homes, cap, LANES), bf16),
            pltpu.VMEM((chunks, 4, resident, 2 * LANES), bf16),
            pltpu.VMEM((chunks, members, LANES, part), bf16),
            pltpu.VMEM((resident, part), f32),
            dma((16,)), dma((24,)), dma((8,)), dma((8,)), dma((chunks + 1,)),
            *ring_sems, *ring_sems, *ring_sems,
            *[dma((chunks, homes))] * 4,
        ],
        compiler_params=pltpu.CompilerParams(
            collective_id=0, has_side_effects=True, vmem_limit_bytes=67043328),
        name="mega",
    )(
        home_tokens,
        mod_weight.reshape(2, members, chunks, LANES, part),
        qkv_weight.reshape(3, members, chunks, LANES, part),
        output_weight.reshape(chunks, LANES, full),
        norm_gain, row_plan.reshape(homes, resident), sample_lengths, modality,
    )


def solution(mesh):
    in_specs = (
        P("dp", "bag"),
        P(None, None, "bag"),
        P(None, None, "bag"),
        P(None, "bag"),
        P("bag", None),
        P(),
        P(),
        P(),
    )
    return jax.shard_map(body, mesh=mesh, in_specs=in_specs, out_specs=P("dp", "bag"), check_vma=False)
```

```python
import functools

import jax
import jax.numpy as jnp
from jax import lax
from jax.experimental import pallas as pl
from jax.experimental.pallas import tpu as pltpu
from jax.sharding import PartitionSpec as P

HD = 64
EPS = 1e-06
LOG2E = 1.4426950408889634


MESH = pl.DeviceIdType.MESH
LANES = 128


def remote(src, dst, send_sem, recv_sem, where):
    return pltpu.make_async_remote_copy(
        src_ref=src, dst_ref=dst, send_sem=send_sem, recv_sem=recv_sem, device_id=where, device_id_type=MESH
    )


class Ring:
    def __init__(self, first, buf, send_sems, recv_sems, places, on_ready):
        self.first, self.buf, self.send_sems, self.recv_sems = first, buf, send_sems, recv_sems
        self.near, self.far, self.twin = places
        self.on_ready = on_ready
        self.half = buf.shape[1] // 2
        self.sent, self.lands = [], {}

    def rows(self, half):
        return pl.ds(half * self.half, self.half)

    def view(self, k, lane, half):
        return self.buf.at[k, self.rows(half), pl.ds(lane * LANES, LANES)]

    def send(self, source, half, k, lane, where):
        copy = remote(source, self.view(k, lane, half), self.send_sems.at[len(self.sent)],
                      self.recv_sems.at[k, lane, half], where)
        copy.start()
        self.sent.append(copy)
        self.lands[k, lane, half] = copy

    def start(self):
        self.send(self.first(0), 0, 3, 0, self.near)
        self.send(self.first(1), 1, 1, 0, self.far)
        self.send(self.first(0), 0, 0, 1, self.twin)
        self.send(self.first(1), 1, 0, 1, self.twin)
        self.send(self.first(1), 1, 3, 0, self.near)
        self.send(self.first(0), 0, 1, 0, self.far)

    def forward(self, k, half):
        self.lands[k, 0, half].wait_recv()
        self.send(self.view(k, 0, half), half, k, 1, self.twin)

    def ready(self, k):
        for half in (0, 1):
            self.lands[k, 1, half].wait_recv()
        self.on_ready(k)

    def relay(self):
        for k, half, where in ((3, 0, self.near), (1, 1, self.far)):
            self.lands[k, 0, half].wait_recv()
            self.send(self.view(k, 0, half), half, 2, 0, where)
            self.send(self.view(k, 0, half), half, k, 1, self.twin)

    def own(self):
        self.ready(0)

    def beside(self):
        self.forward(3, 1)
        self.forward(1, 0)
        self.ready(3)
        self.ready(1)

    def across(self):
        self.forward(2, 0)
        self.forward(2, 1)

    def last(self):
        self.ready(2)

    def finish(self):
        for copy in self.sent:
            copy.wait_send()


def loop(begin, end, step):
    def run(index, carry):
        step(index)
        return carry

    lax.fori_loop(begin, end, run, 0)


def head_scale(x, gain):
    low = lax.broadcasted_iota(jnp.int32, x.shape, 1) < HD

    def mean(t):
        left = jnp.sum(jnp.where(low, t, 0.0), axis=1, keepdims=True)
        right = jnp.sum(jnp.where(low, 0.0, t), axis=1, keepdims=True)
        return jnp.where(low, left, right) * (1.0 / HD)

    shifted = x - mean(x)
    return (shifted * lax.rsqrt(mean(shifted * shifted) + EPS) * gain).astype(jnp.bfloat16)


def extend(x, sample, keep_low):
    lane = lax.broadcasted_iota(jnp.int32, x.shape, 1)
    mark = jnp.where((lane % HD) == sample, 128.0, 0.0).astype(x.dtype)
    return jnp.where((lane < HD) == keep_low, x, mark)


def mega_kernel(
    homes_x, homes_y,
    tokens, modw, qkvw, outw, gain, raw_plan, lengths, modality,
    out,
    own_row, table, cols, keys, plan, buf1, w1, acc1, proj, sbuf, abuf, buf2, w2, acc2, acc_pick, hots, qx, kx, vx, ahead, att, back, buf3, w3, acc3,
    sem_w1, sem_w2, sem_w3s, sem_w3r, sem_own,
    s1, r1, s2, r2, s3, r3, sa, ra, sb, rb,
):
    homes = homes_x * homes_y
    me = lax.axis_index("dp")
    bag = lax.axis_index("bag")
    x, y = lax.div(me, homes_y), lax.rem(me, homes_y)
    z, core = lax.div(bag, 2), lax.rem(bag, 2)
    resident, part = tokens.shape
    pack = buf2.shape[2]
    cap = sbuf.shape[2]
    chunks = part // LANES
    f32, bf16 = jnp.float32, jnp.bfloat16

    def member(k, lane):
        return lax.rem(z + k, 4) * 2 + (core if lane == 0 else 1 - core)

    def home(turn, sign):
        step = lax.rem(turn * 5, homes)
        dx, dy = lax.div(step, homes_y), lax.rem(step, homes_y)
        if sign < 0:
            dx, dy = homes_x - dx, homes_y - dy
        return lax.rem(x + dx, homes_x) * homes_y + lax.rem(y + dy, homes_y)

    places = ({"bag": member(1, 0)}, {"bag": member(3, 0)}, {"bag": member(0, 1)})

    w1_loads, w2_loads = [], []
    for k in (0, 3, 1, 2):
        for lane in (0, 1):
            for m in range(2):
                w1_loads.append(pltpu.make_async_copy(
                    modw.at[m, member(k, lane)],
                    w1.at[:, k * 2 + lane, :, pl.ds(m * part, part)], sem_w1.at[len(w1_loads)]))
            for m in range(3):
                w2_loads.append(pltpu.make_async_copy(
                    qkvw.at[m, member(k, lane)],
                    w2.at[:, k * 2 + lane, :, pl.ds(m * part, part)], sem_w2.at[len(w2_loads)]))
    own_loads = [
        pltpu.make_async_copy(tokens.at[:, pl.ds(c * LANES, LANES)],
                              buf1.at[c, 0, :, pl.ds(0, LANES)], sem_own.at[c])
        for c in range(chunks)
    ]
    for load in own_loads + w1_loads:
        load.start()

    barrier = pltpu.get_barrier_semaphore()
    for turn in range(1, homes):
        pl.semaphore_signal(barrier, inc=1, device_id={"dp": home(turn, 1)}, device_id_type=MESH)
    for step in range(1, 8):
        pl.semaphore_signal(barrier, inc=1, device_id={"bag": lax.rem(bag + step, 8)}, device_id_type=MESH)
    pl.semaphore_wait(barrier, homes - 1 + 7)

    def bag_block(index):
        return hots.at[index]

    def home_block(index):
        return buf1.at[lax.div(index, 4), lax.rem(index, 4)]

    def spread(block, hot):
        def one(index):
            block(index)[...] = jnp.concatenate([hot(2 * index), hot(2 * index + 1)], axis=1)

        loop(0, homes // 2, one)

    def bag_hot(turn):
        ids = lax.broadcasted_iota(jnp.int32, (pack, cap), 0)
        return (ids == table[pl.ds(home(turn, -1), 1), :]).astype(bf16)

    def home_hot(turn):
        ids = lax.broadcasted_iota(jnp.int32, (resident, cap), 1) + home(turn, -1) * cap
        return (ids == cols[pl.ds(0, resident), 1:2]).astype(bf16)

    def split(rows):
        bags = ((rows.astype(f32) + 0.5) * (1.0 / pack)).astype(jnp.int32)
        return bags, rows - bags * pack

    def ends_of(index):
        ends = [lengths[0, index]]
        for sample in range(1, lengths.shape[0]):
            ends.append(ends[-1] + lengths[sample, index])
        return ends

    def contract(left, right):
        return lax.dot_general(left, right, (((1,), (1,)), ((), ())), preferred_element_type=f32)

    def tables():
        for piece in range(resident // 256):
            before = lax.broadcasted_iota(jnp.int32, (resident, 256), 0)
            after = lax.broadcasted_iota(jnp.int32, (resident, 256), 1) + piece * 256
            hots[piece, 0:resident, :] = (before < after).astype(bf16)
        pieces = resident // LANES

        def line_up(index):
            plan[pl.ds(index, 1), :] = jnp.concatenate(
                [raw_plan[pl.ds(index * pieces + piece, 1), :] for piece in range(pieces)], axis=1)

        loop(0, homes, line_up)
        bags, _ = split(plan[...])
        own_bag, own_slot = split(plan[pl.ds(me, 1), :])
        mine = bags == me
        each = own_bag == lax.broadcasted_iota(jnp.int32, (homes, resident), 0)
        both = jnp.concatenate([mine.astype(bf16), each.astype(bf16)], axis=0)
        ranks = jnp.concatenate(
            [jnp.dot(both, hots[piece, 0:resident, :], preferred_element_type=f32)
             for piece in range(resident // 256)], axis=1)
        keys[...] = jnp.where(mine, ranks[:homes].astype(jnp.int32), -1)
        place = jnp.sum(jnp.where(each, ranks[homes:], 0.0), axis=0, keepdims=True).astype(jnp.int32)
        own_row[...] = own_bag * cap + place
        kind = jnp.zeros_like(own_bag)
        for index in range(homes):
            ends = ends_of(index)
            value = jnp.full_like(own_bag, 0) + modality[len(ends) - 1, index]
            for sample in range(len(ends) - 2, -1, -1):
                value = jnp.where(own_slot < ends[sample], modality[sample, index], value)
            kind = jnp.where(own_bag == index, value, kind)
        line = lax.broadcasted_iota(jnp.int32, (8, resident), 0)
        facts = jnp.where(line == 0, own_bag, jnp.where(line == 1, place, kind)).astype(bf16)

        def same(index):
            at = pl.multiple_of(index * 128, 128)
            own = lax.broadcasted_iota(jnp.int32, (128, resident), 0) + at
            hot = (own == lax.broadcasted_iota(jnp.int32, (128, resident), 1)).astype(bf16)
            got = contract(hot, facts).astype(jnp.int32)
            cols[pl.ds(at, 128), 1:2] = got[:, 0:1] * cap + got[:, 1:2]
            cols[pl.ds(at, 128), 2:3] = got[:, 2:3]

        loop(0, resident // 128, same)

        def slots_of(index):
            _, slot = split(plan[pl.ds(index, 1), :])
            high = lax.shift_right_logical(slot, 8)
            parts = jnp.where(line == 0, high, jnp.where(line == 1, slot - high * 256, 1)).astype(bf16)
            hot = (lax.broadcasted_iota(jnp.int32, (cap, resident), 0) == keys[pl.ds(index, 1), :]).astype(bf16)
            row = contract(parts, hot).astype(jnp.int32)
            table[pl.ds(index, 1), :] = jnp.where(row[2:3] > 0, row[0:1] * 256 + row[1:2], -1)
            col = contract(hot, parts).astype(jnp.int32)
            at = pl.multiple_of(index * cap, cap)
            cols[pl.ds(at, cap), 0:1] = jnp.where(col[:, 2:3] > 0, col[:, 0:1] * 256 + col[:, 1:2], -1)

        loop(0, homes, slots_of)
        here = lax.broadcasted_iota(jnp.int32, (pack, 1), 0)
        sample = jnp.zeros_like(here)
        for end in ends_of(me):
            sample = sample + (here >= end).astype(jnp.int32)
        cols[pl.ds(0, pack), 3:4] = sample

    half1 = resident // 2

    def project(c, k):
        def tile(index):
            lanes = pl.ds(pl.multiple_of(index * 256, 256), 256)
            weight = w1[c, pl.ds(2 * k, 2), :, lanes].reshape(2 * LANES, 256)
            value = jnp.dot(buf1[c, k], weight, preferred_element_type=f32)
            if c == 0 and k == 0:
                acc1[:, lanes] = value
            else:
                acc1[:, lanes] += value

        loop(0, 2 * part // 256, tile)

    rings = [
        Ring(lambda half, c=c: tokens.at[pl.ds(half * half1, half1), pl.ds(c * LANES, LANES)],
             buf1.at[c], s1.at[c], r1.at[c], places, lambda k, c=c: project(c, k))
        for c in range(chunks)
    ]
    for ring in rings:
        ring.start()
    tables()
    for load in own_loads + w1_loads:
        load.wait()
    for load in w2_loads:
        load.start()
    rings[0].own()
    spread(bag_block, bag_hot)
    rings[0].relay()
    rings[1].own()
    rings[1].relay()
    rings[0].beside()
    rings[2].own()
    rings[2].relay()
    rings[1].beside()
    rings[0].across()
    rings[2].beside()
    rings[1].across()
    rings[0].last()
    rings[1].last()
    rings[2].across()
    rings[2].last()
    is_first = cols[pl.ds(0, resident), 2:3] == 0
    proj[...] = jnp.where(is_first, acc1[:, :part], acc1[:, part:]).astype(bf16)

    def to_bag(c, turn):
        return remote(sbuf.at[c, turn], abuf.at[c, turn], sa.at[c, turn], ra.at[c, turn], {"dp": home(turn, 1)})

    def to_home(c, turn):
        return remote(sbuf.at[c, turn], back.at[c, turn], sb.at[c, turn], rb.at[c, turn], {"dp": home(turn, 1)})

    def stay(c, target, sem):
        return pltpu.make_async_copy(sbuf.at[c, 0], target.at[c, 0], sem.at[c, 0])

    group = 4

    def launch(c, index, copy, target, sem):
        for j in range(group):
            if j == 0:
                @pl.when(index == 0)
                def _():
                    stay(c, target, sem).start()

                @pl.when(index > 0)
                def _():
                    copy(c, index * group).start()
            else:
                copy(c, index * group + j).start()

    def fill(first, last):
        def some(index):
            hots = []
            for j in range(group):
                ids = lax.broadcasted_iota(jnp.int32, (cap, resident), 0) + home(index * group + j, 1) * cap
                hots.append((own_row[...] == ids).astype(bf16))
            block = jnp.dot(jnp.concatenate(hots, axis=0), proj[:, first * LANES:last * LANES],
                            preferred_element_type=f32).astype(bf16)
            for c in range(first, last):
                for j in range(group):
                    sbuf[c, index * group + j] = block[j * cap:(j + 1) * cap, (c - first) * LANES:(c - first + 1) * LANES]
                if c == first:
                    launch(c, index, to_bag, abuf, ra)

        loop(0, homes // group, some)

    def columns(index):
        return outw.at[:, :, pl.ds(pl.multiple_of(index * part, part), part)]

    w3_own = pltpu.make_async_copy(columns(bag), w3.at[:, 0], sem_own.at[chunks])
    w3_copies = []

    def share(*blocks):
        for k, lane in blocks:
            if k or lane:
                target = lax.rem(z + 4 - k, 4) * 2 + (core if lane == 0 else 1 - core)
                index = k * 2 + lane
                copy = remote(columns(target), w3.at[:, index], sem_w3s.at[index], sem_w3r.at[index],
                              {"bag": target})
                copy.start()
                w3_copies.append(copy)

    fill(0, 1)
    share((1, 0), (3, 0), (0, 1))
    fill(1, chunks)
    for c in range(2, chunks):
        loop(0, homes // group, lambda index, c=c: launch(c, index, to_bag, abuf, ra))
    for ring in rings:
        ring.finish()

    def collect(c, source, sem, copy, rows, block):
        acc_pick[pl.ds(0, rows), :] = jnp.zeros((rows, LANES), f32)

        def take(index):
            values = []
            for j in range(group):
                turn = index * group + j
                if j == 0:
                    @pl.when(index == 0)
                    def _():
                        stay(c, source, sem).wait()

                    @pl.when(index > 0)
                    def _():
                        copy(c, turn).wait_recv()
                else:
                    copy(c, turn).wait_recv()
                values.append(source[c, turn])
            hot = jnp.concatenate([block(2 * index)[...], block(2 * index + 1)[...]], axis=1)
            acc_pick[pl.ds(0, rows), :] += jnp.dot(
                hot, jnp.concatenate(values, axis=0), preferred_element_type=f32)

        loop(0, homes // group, take)
        return acc_pick[pl.ds(0, rows), :].astype(bf16)

    half2 = pack // 2

    def qkv(c, k):
        def tile(index):
            rows = pl.ds(pl.multiple_of(index * half2, half2), half2)
            weight = w2[c, pl.ds(2 * k, 2)].reshape(2 * LANES, 3 * part)
            value = jnp.dot(buf2[c, k, rows, :], weight, preferred_element_type=f32)
            if c == 0 and k == 0:
                acc2[rows, :] = value
            else:
                acc2[rows, :] += value

        loop(0, 2, tile)

    rings = [
        Ring(lambda half, c=c: buf2.at[c, 0, pl.ds(half * half2, half2), pl.ds(0, LANES)],
             buf2.at[c], s2.at[c], r2.at[c], places, lambda k, c=c: qkv(c, k))
        for c in range(chunks)
    ]

    def return_hot(turn):
        ids = lax.broadcasted_iota(jnp.int32, (cap, pack), 1)
        hot = (cols[pl.ds(pl.multiple_of(home(turn, 1) * cap, cap), cap), 0:1] == ids).astype(bf16)
        begin = lax.rem(turn, 2) * (pack // 2)
        for piece in range(pack // 256):
            rows = pl.ds(pl.multiple_of(begin + piece * cap, cap), cap)
            hots[lax.div(turn, 2), rows, :] = hot[:, piece * 256:(piece + 1) * 256]

    def pack_in(c):
        buf2[c, 0, :, 0:LANES] = collect(c, abuf, ra, to_bag, pack, bag_block)
        rings[c].start()

    pack_in(0)
    spread(home_block, home_hot)
    pack_in(1)
    rings[0].relay()
    for load in w2_loads:
        load.wait()
    rings[0].own()
    pack_in(2)
    loop(0, homes, return_hot)
    rings[1].relay()
    rings[1].own()
    rings[0].beside()
    rings[2].own()
    rings[1].beside()
    rings[0].across()
    rings[2].relay()
    rings[0].last()
    rings[2].beside()
    rings[1].across()
    rings[1].last()
    rings[2].across()
    rings[2].last()
    for c in range(chunks):
        stay_turns = lambda turn, c=c: to_bag(c, turn).wait_send()
        loop(1, homes, stay_turns)
    for ring in rings:
        ring.finish()

    blocks = 5
    block_rows = pack // blocks

    def prepare(pair):
        key = head_scale(acc2[:, pl.ds(part + pair * LANES, LANES)], gain[1:2, pl.ds(pair * LANES, LANES)])
        value = acc2[:, pl.ds(2 * part + pair * LANES, LANES)].astype(bf16)
        low = lax.broadcasted_iota(jnp.int32, value.shape, 1) < HD
        query = head_scale(acc2[:, pl.ds(pair * LANES, LANES)], gain[0:1, pl.ds(pair * LANES, LANES)])
        for head in range(2):
            qx[head] = extend(query, cols[pl.ds(0, pack), 3:4], head == 0)
            kx[head] = extend(key, cols[pl.ds(0, pack), 3:4], head == 0)
            vx[head] = jnp.where(low == (head == 0), value, jnp.ones_like(value))
        ahead[...] = score(0, 0)

    def score(head, index):
        rows = pl.ds(pl.multiple_of(index * block_rows, block_rows), block_rows)
        return lax.dot_general(qx[head, rows, :], kx[head], (((1,), (1,)), ((), ())), preferred_element_type=f32)

    def weigh(head, s):
        top = jnp.max(s, axis=1, keepdims=True)
        p = jnp.exp2((s - top) * (LOG2E * HD ** -0.5)).astype(bf16)
        o = jnp.dot(p, vx[head], preferred_element_type=f32)
        return o / pltpu.roll(o, HD, 1)

    def attend(index):
        rows = pl.ds(pl.multiple_of(index * block_rows, block_rows), block_rows)
        odd_scores = score(1, index)
        even = weigh(0, ahead[...])
        ahead[...] = score(0, lax.rem(index + 1, blocks))
        odd = weigh(1, odd_scores)
        low = lax.broadcasted_iota(jnp.int32, even.shape, 1) < HD
        att[rows, :] = jnp.where(low, even, odd).astype(bf16)

    pieces = pack // 256

    def send_back(c):
        def some(index):
            total = None
            for piece in range(pieces):
                left = jnp.concatenate(
                    [hots[2 * index + j // 2, pl.ds(((j % 2) * pieces + piece) * cap, cap), :] for j in range(group)],
                    axis=0)
                value = jnp.dot(left, att[pl.ds(piece * 256, 256), :], preferred_element_type=f32)
                total = value if total is None else total + value
            block = total.astype(bf16)
            for j in range(group):
                sbuf[c, index * group + j] = block[j * cap:(j + 1) * cap]
            launch(c, index, to_home, back, rb)

        loop(0, homes // group, some)

    def finish(c, k):
        weight = w3[c, pl.ds(2 * k, 2)].reshape(2 * LANES, part)
        value = jnp.dot(buf3[c, k], weight, preferred_element_type=f32)
        if c == 0 and k == 0:
            acc3[...] = value
        elif c == chunks - 1 and k == 2:
            out[...] = (acc3[...] + value).astype(bf16)
        else:
            acc3[...] += value

    rings = [
        Ring(lambda half, c=c: buf3.at[c, 0, pl.ds(half * half1, half1), pl.ds(0, LANES)],
             buf3.at[c], s3.at[c], r3.at[c], places, lambda k, c=c: finish(c, k))
        for c in range(chunks)
    ]

    def home_in(c):
        buf3[c, 0, :, 0:LANES] = collect(c, back, rb, to_home, resident, home_block)
        rings[c].start()

    prepare(0)
    loop(0, 1, attend)
    w3_own.start()
    share((2, 0), (2, 1), (1, 1), (3, 1))
    loop(1, blocks, attend)
    send_back(0)
    prepare(1)
    loop(0, blocks, attend)
    send_back(1)
    home_in(0)
    prepare(2)
    loop(0, 3, attend)
    rings[0].relay()
    home_in(1)
    loop(3, blocks, attend)
    send_back(2)
    rings[1].relay()
    w3_own.wait()
    for copy in w3_copies:
        copy.wait()
    rings[0].own()
    rings[0].beside()
    rings[0].across()
    rings[1].own()
    rings[0].last()
    home_in(2)
    rings[1].beside()
    rings[1].across()
    rings[2].own()
    rings[1].last()
    rings[2].relay()
    rings[2].beside()
    rings[2].across()
    rings[2].last()
    for c in range(chunks):
        loop(1, homes, lambda turn, c=c: to_home(c, turn).wait_send())
    for ring in rings:
        ring.finish()


def body(
    home_tokens,
    mod_weight,
    qkv_weight,
    norm_gain,
    output_weight,
    row_plan,
    sample_lengths,
    modality,
):
    homes = lax.axis_size("dp")
    resident, part = home_tokens.shape
    full = mod_weight.shape[1]
    pack = resident + resident // 4
    cap = 2 * resident // homes
    slots = cap * homes
    bf16, f32 = jnp.bfloat16, jnp.float32
    any_spec = pl.BlockSpec(memory_space=pl.ANY)
    vmem = pl.BlockSpec(memory_space=pltpu.VMEM)
    smem = pl.BlockSpec(memory_space=pltpu.SMEM)
    dma = pltpu.SemaphoreType.DMA
    chunks = part // LANES
    members = full // part
    kernel = functools.partial(mega_kernel, 4, 4)
    ring_sems = [dma((chunks, 14)), dma((chunks, 4, 2, 2))]
    return pl.pallas_call(
        kernel,
        out_shape=jax.ShapeDtypeStruct((resident, part), bf16),
        in_specs=[any_spec] * 4 + [vmem] * 2 + [smem] * 2,
        out_specs=vmem,
        scratch_shapes=[
            pltpu.VMEM((1, resident), jnp.int32),
            pltpu.VMEM((homes, cap), jnp.int32),
            pltpu.VMEM((slots, 4), jnp.int32),
            pltpu.VMEM((homes, resident), jnp.int32),
            pltpu.VMEM((homes, resident), jnp.int32),
            pltpu.VMEM((chunks, 4, resident, 2 * LANES), bf16),
            pltpu.VMEM((chunks, members, LANES, 2 * part), bf16),
            pltpu.VMEM((resident, 2 * part), f32),
            pltpu.VMEM((resident, part), bf16),
            pltpu.VMEM((chunks, homes, cap, LANES), bf16),
            pltpu.VMEM((chunks, homes, cap, LANES), bf16),
            pltpu.VMEM((chunks, 4, pack, 2 * LANES), bf16),
            pltpu.VMEM((chunks, members, LANES, 3 * part), bf16),
            pltpu.VMEM((pack, 3 * part), f32),
            pltpu.VMEM((pack, LANES), f32),
            pltpu.VMEM((homes // 2, pack, 2 * LANES), bf16),
            pltpu.VMEM((2, pack, LANES), bf16),
            pltpu.VMEM((2, pack, LANES), bf16),
            pltpu.VMEM((2, pack, LANES), bf16),
            pltpu.VMEM((pack // 5, pack), f32),
            pltpu.VMEM((pack, LANES), bf16),
            pltpu.VMEM((chunks, homes, cap, LANES), bf16),
            pltpu.VMEM((chunks, 4, resident, 2 * LANES), bf16),
            pltpu.VMEM((chunks, members, LANES, part), bf16),
            pltpu.VMEM((resident, part), f32),
            dma((16,)), dma((24,)), dma((8,)), dma((8,)), dma((chunks + 1,)),
            *ring_sems, *ring_sems, *ring_sems,
            *[dma((chunks, homes))] * 4,
        ],
        compiler_params=pltpu.CompilerParams(
            collective_id=0, has_side_effects=True, vmem_limit_bytes=67043328),
        name="mega",
    )(
        home_tokens,
        mod_weight.reshape(2, members, chunks, LANES, part),
        qkv_weight.reshape(3, members, chunks, LANES, part),
        output_weight.reshape(chunks, LANES, full),
        norm_gain, row_plan.reshape(-1, LANES), sample_lengths.T, modality.T,
    )


def solution(mesh):
    in_specs = (
        P("dp", "bag"),
        P(None, None, "bag"),
        P(None, None, "bag"),
        P(None, "bag"),
        P("bag", None),
        P(),
        P(),
        P(),
    )
    return jax.shard_map(body, mesh=mesh, in_specs=in_specs, out_specs=P("dp", "bag"), check_vma=False)
```
